256 devices in a mesh: tm: 4 (over z_lo, core), vocab: 64 (over x, y, z_hi).
Axes of the slice: x: 4, y: 4, z: 8 (z_hi: 4, z_lo: 2; z = z_hi * 2 + z_lo), core: 2. Of those that a mesh axis runs over, the one named last changes fastest.
Arguments:
- frames: bfloat16 [6144, 1024], P(('tm', 'vocab')), may hold values from -6 to 6
- qkv_weight: bfloat16 [1024, 3072], replicated, may hold values from -0.375 to 0.375
- attn_out_weight: bfloat16 [1024, 1024], replicated, may hold values from -0.1875 to 0.1875
- head_weight: bfloat16 [1024, 131072], P('tm', 'vocab'), may hold values from -0.5 to 0.5
- back_weight: bfloat16 [131072, 1024], P('vocab', 'tm'), may hold values from -6 to 6
Outputs:
- conditioned: bfloat16 [6144, 1024], P(('tm', 'vocab'))
- log_norm: float32 [6144], P(('tm', 'vocab'))
The draws below stay inside these ranges and needn't reach their ends.
All inputs are finite; a program needn't handle non-finite values.
Results may differ from the reference program's by a relative error of at most 0.017.
The reference program's roundings to bfloat16 on the way (of `normed`, `project`, `weights`, `context`, `hidden`, `unit` and `label_probs`) count: a program that leaves them out, or rounds other values in their place, can miss the bound.
Values may be sent and summed in bfloat16 or wider, within the bound.
No kernel may reach another device: no remote copies, remote signals or barrier semaphores. Data moves between devices by JAX's collectives and lax.ppermute only.
A program may use at most 128 MiB of HBM per device.

```python
import math
import jax
import jax.numpy as jnp
from jax import lax

D = 1024
HEADS = 16
HEAD_DIM = 64
WIN = 128
FR_DEV = 24
VOCAB = 131072
TOKENS = 6144
N_VOCAB = 64


def draw_qkv_weight(key, part):
    base_draw = jnp.clip(jax.random.normal(key, (D, 3 * D), jnp.float32), -4.0, 4.0)
    column_index = jnp.arange(3 * D, dtype=jnp.int32)
    column_scale = jnp.where(column_index < 2 * D, 3.0, 1.0) / math.sqrt(D)
    return (base_draw * column_scale[None, :]).astype(jnp.bfloat16)


def level_of(own_key, shape, shards, low, high):
    def one(dim, parts):
        steps = jax.random.uniform(jax.random.fold_in(jax.random.fold_in(own_key, 6), dim), (parts,), jnp.float32, low / len(shards), high / len(shards))
        return jnp.repeat(jnp.exp(steps), shape[dim] // parts).reshape((-1,) + (1,) * (len(shape) - dim - 1))

    level = one(*shards[0])
    for cut in shards[1:]:
        level = level * one(*cut)
    return level


def bell_draw(stream_key, shape, scale, reach, shards=(), kind=jnp.bfloat16):
    values = scale * jax.random.normal(stream_key, shape, jnp.float32)
    if shards:
        values = values * level_of(stream_key, shape, shards, -0.22, 0.18)
    return jnp.clip(values, -reach, reach).astype(kind)


def setup_inputs(seed: int = 0) -> dict:
    keys = jax.random.split(jax.random.key(seed), 6)
    return {
        "frames": bell_draw(keys[0], (TOKENS, D), 1.0, 6.0, ((0, 256),)),
        "qkv_weight": draw_qkv_weight(jax.random.fold_in(keys[5], 71), 0),
        "attn_out_weight": bell_draw(keys[2], (D, D), D ** -0.5, 0.1875),
        "head_weight": bell_draw(keys[3], (D, VOCAB), (D // 9) ** -0.5, 0.5, ((0, 4), (1, 64))),
        "back_weight": bell_draw(keys[4], (VOCAB, D), 1.0, 6.0, ((0, 64), (1, 4))),
    }


def root_norm(values):
    return values * lax.rsqrt(lax.optimization_barrier(jnp.mean(values * values, axis=-1, keepdims=True)) + 1e-06)

def reference(frames, qkv_weight, attn_out_weight, head_weight, back_weight):
    total_frames = frames.shape[0]
    model_width = frames.shape[1]
    normed = root_norm(frames.astype(jnp.float32)).astype(jnp.bfloat16)
    project = jnp.dot(normed, qkv_weight, preferred_element_type=jnp.float32).astype(jnp.bfloat16)
    query = project[:, :model_width].reshape(total_frames, HEADS, HEAD_DIM)
    padded = jnp.concatenate([jnp.zeros((WIN, 2 * model_width), jnp.bfloat16), project[:, model_width:]], axis=0)

    def attend(block_id):
        first = block_id * WIN
        query_blk = lax.dynamic_slice_in_dim(query, first, WIN, 0).astype(jnp.float32)
        pair_blk = lax.dynamic_slice_in_dim(padded, first, 2 * WIN, 0)
        key_blk = pair_blk[:, :model_width].reshape(2 * WIN, HEADS, HEAD_DIM).astype(jnp.float32)
        value_blk = pair_blk[:, model_width:].reshape(2 * WIN, HEADS, HEAD_DIM).astype(jnp.float32)
        scores = jnp.einsum('qhd,khd->hqk', query_blk, key_blk) / math.sqrt(HEAD_DIM)
        scores = 50.0 * jnp.tanh(scores / 50.0)
        query_pos = first + jnp.arange(WIN, dtype=jnp.int32)
        key_pos = first - WIN + jnp.arange(2 * WIN, dtype=jnp.int32)
        allowed = (key_pos[None, :] <= query_pos[:, None]) & (key_pos[None, :] > query_pos[:, None] - WIN) & (key_pos[None, :] >= 0)
        expo = jnp.where(allowed[None], jnp.exp(scores), 0.0)
        weights = (expo / lax.optimization_barrier(jnp.sum(expo, axis=-1, keepdims=True))).astype(jnp.bfloat16)
        context = jnp.einsum('hqk,khd->qhd', weights.astype(jnp.float32), value_blk)
        return context.astype(jnp.bfloat16).reshape(WIN, model_width)
    context = lax.map(attend, jnp.arange(total_frames // WIN, dtype=jnp.int32)).reshape(total_frames, model_width)
    hidden = (frames.astype(jnp.float32) + jnp.dot(context, attn_out_weight, preferred_element_type=jnp.float32)).astype(jnp.bfloat16)
    unit = root_norm(hidden.astype(jnp.float32)).astype(jnp.bfloat16)
    group = FR_DEV * N_VOCAB

    def head_block(block_id):
        rows_blk = lax.dynamic_slice_in_dim(unit, block_id * group, group, 0)
        logits = jnp.dot(rows_blk, head_weight, preferred_element_type=jnp.float32)
        logits = 30.0 * jnp.tanh(logits / 30.0)
        label_probs = jnp.exp(logits).astype(jnp.bfloat16)
        totals = lax.optimization_barrier(jnp.sum(label_probs.astype(jnp.float32), axis=-1))
        partial_value = jnp.dot(label_probs, back_weight, preferred_element_type=jnp.float32)
        return (partial_value / totals[:, None], jnp.log(totals))
    back_proj, log_norm = lax.map(head_block, jnp.arange(total_frames // group, dtype=jnp.int32))
    back_proj = back_proj.reshape(total_frames, model_width)
    log_norm = log_norm.reshape(total_frames)
    center = back_proj - lax.optimization_barrier(jnp.mean(back_proj, axis=-1, keepdims=True))
    spread = lax.optimization_barrier(jnp.mean(center * center, axis=-1, keepdims=True))
    conditioned = (hidden.astype(jnp.float32) + center * lax.rsqrt(spread + 1e-05)).astype(jnp.bfloat16)
    return (conditioned, log_norm)
```

```python
import math

import jax
import jax.numpy as jnp
from jax import lax
from jax.sharding import Mesh, PartitionSpec as P

HEADS = 16
HEAD_DIM = 64
WIN = 128
BF = jnp.bfloat16
F32 = jnp.float32
TIME = ("zl", "c")
PLANE = ("x", "y")
COL = "zh"
BLOCKS = TIME + PLANE
EVERY = BLOCKS + (COL,)


def gathered(block, axes):
    size = lax.axis_size(axes)
    copies = lax.optimization_barrier(jnp.broadcast_to(block[None], (size,) + block.shape))
    parts = lax.all_to_all(copies, axes, 0, 0)
    return parts.reshape((size * block.shape[0],) + block.shape[1:])


def passed_along(block, axes, distance):
    devices = range(lax.axis_size(axes))
    route = [(i, i + distance) for i in devices if i + distance in devices]
    return lax.ppermute(block, axes, route)


def root_norm(values):
    return values * lax.rsqrt(jnp.mean(values * values, axis=-1, keepdims=True) + 1e-06)


def body(frames, qkv_weight, attn_out_weight, head_weight, back_weight):
    rows = frames.shape[0]
    width = frames.shape[1]
    planes = lax.axis_size(PLANE)
    cols = lax.axis_size(COL)
    block = rows * cols
    far = WIN - block
    full_head = lax.all_gather(head_weight, TIME, axis=0, tiled=True)
    full_back = lax.all_gather(back_weight, TIME, axis=1, tiled=True)

    own = gathered(frames, COL)
    prev = passed_along(own, BLOCKS, 1)
    prev2 = passed_along(own[block - far :], BLOCKS, 2)
    keys = WIN + block
    normed = root_norm(jnp.concatenate([prev2, prev, own], axis=0).astype(F32)).astype(BF)
    project = jnp.dot(normed, qkv_weight, preferred_element_type=F32).astype(BF)
    query = project[WIN:, :width].reshape(block, HEADS, HEAD_DIM)
    key_part = project[:, width : 2 * width].reshape(keys, HEADS, HEAD_DIM)
    value_part = project[:, 2 * width :].reshape(keys, HEADS, HEAD_DIM)
    first = lax.axis_index(BLOCKS) * block
    query_pos = first + jnp.arange(block, dtype=jnp.int32)
    key_pos = first - WIN + jnp.arange(keys, dtype=jnp.int32)
    scores = jnp.einsum(
        "qhd,khd->hqk", query, key_part, preferred_element_type=F32
    ) / math.sqrt(HEAD_DIM)
    scores = 50.0 * jnp.tanh(scores / 50.0)
    allowed = (
        (key_pos[None, :] <= query_pos[:, None])
        & (key_pos[None, :] > query_pos[:, None] - WIN)
        & (key_pos[None, :] >= 0)
    )
    expo = jnp.where(allowed[None], jnp.exp(scores), 0.0)
    weights = (expo / jnp.sum(expo, axis=-1, keepdims=True)).astype(BF)
    context = jnp.einsum("hqk,khd->qhd", weights, value_part, preferred_element_type=F32)
    context = context.astype(BF).reshape(block, width)
    hidden = (
        own.astype(F32) + jnp.dot(context, attn_out_weight, preferred_element_type=F32)
    ).astype(BF)
    unit = root_norm(hidden.astype(F32)).astype(BF)

    logits = jnp.dot(gathered(unit, PLANE), full_head, preferred_element_type=F32)
    label_probs = jnp.exp(30.0 * jnp.tanh(logits / 30.0)).astype(BF)
    totals = jnp.sum(label_probs.astype(F32), axis=-1)
    partial = jnp.dot(label_probs, full_back, preferred_element_type=F32)

    high = lax.reduce_precision(totals, 8, 7)
    mid = lax.reduce_precision(totals - high, 8, 7)
    low = totals - high - mid
    split = jnp.stack([high, mid, low]).astype(BF).reshape(3, planes, block)
    split = jnp.pad(split.transpose(1, 0, 2), ((0, 0), (0, 5), (0, width - block)))
    sent = jnp.concatenate([partial.astype(BF).reshape(planes, block, width), split], axis=1)
    summed = jnp.sum(lax.all_to_all(sent, PLANE, 0, 0).astype(F32), axis=0)
    block_totals = jnp.sum(summed[block : block + 3, :block], axis=0)
    high = lax.reduce_precision(block_totals, 8, 7)
    mid = lax.reduce_precision(block_totals - high, 8, 7)
    low = block_totals - high - mid
    split = jnp.stack([high, mid, low]).astype(BF).reshape(3, cols, rows)
    split = jnp.pad(split.transpose(1, 0, 2), ((0, 0), (0, 5), (0, width - rows)))
    sent = jnp.concatenate([summed[:block].astype(BF).reshape(cols, rows, width), split], axis=1)
    summed = jnp.sum(lax.all_to_all(sent, COL, 0, 0).astype(F32), axis=0)
    owned_totals = jnp.sum(summed[rows : rows + 3, :rows], axis=0)
    back_proj = summed[:rows] / owned_totals[:, None]

    own_hidden = lax.dynamic_slice_in_dim(hidden, lax.axis_index(COL) * rows, rows, 0)
    center = back_proj - jnp.mean(back_proj, axis=-1, keepdims=True)
    spread = jnp.mean(center * center, axis=-1, keepdims=True)
    conditioned = (own_hidden.astype(F32) + center * lax.rsqrt(spread + 1e-05)).astype(BF)
    return (conditioned, jnp.log(owned_totals))


def solution(mesh):
    cube = Mesh(mesh.devices.reshape(2, 2, 4, 4, 4), EVERY)
    return jax.shard_map(
        body,
        mesh=cube,
        in_specs=(P(EVERY, None), P(), P(), P(TIME, PLANE + (COL,)), P(PLANE + (COL,), TIME)),
        out_specs=(P(EVERY, None), P(EVERY)),
        check_vma=False,
    )
```

```python
import math

import jax
import jax.numpy as jnp
from jax import lax
from jax.sharding import Mesh, PartitionSpec as P


HEADS = 16
HEAD_DIM = 64
WIN = 128
BF = jnp.bfloat16
F32 = jnp.float32
TIME = ("zl", "c")
PLANE = ("x", "y")
COL = "zh"
BLOCKS = TIME + PLANE
EVERY = BLOCKS + (COL,)
CHUNKS = ((0, 16), (16, 24))


def gathered(block, axes):
    size = lax.axis_size(axes)
    copies = lax.optimization_barrier(jnp.broadcast_to(block[None], (size,) + block.shape))
    parts = lax.all_to_all(copies, axes, 0, 0)
    return parts.reshape((size * block.shape[0],) + block.shape[1:])


def passed_along(block, axes, distance):
    devices = range(lax.axis_size(axes))
    route = [(i, i + distance) for i in devices if i + distance in devices]
    return lax.ppermute(block, axes, route)


def swapped(block, axis):
    return lax.ppermute(block, axis, [(0, 1), (1, 0)])


def over_time(block, axis):
    beside = swapped(block, "c")
    across = swapped(block, "zl")
    corner = swapped(across, "c")
    return jnp.concatenate([block, beside, across, corner], axis=axis)


def from_own(values):
    quarter = values.shape[1] // 4
    q = [values[:, i * quarter : (i + 1) * quarter] for i in range(4)]
    odd = lax.axis_index("c") == 1
    q = [jnp.where(odd, q[i ^ 1], q[i]) for i in range(4)]
    late = lax.axis_index("zl") == 1
    return jnp.concatenate([jnp.where(late, q[i ^ 2], q[i]) for i in range(4)], axis=1)


def three_rows(totals, width):
    high = lax.reduce_precision(totals, 8, 7)
    mid = lax.reduce_precision(totals - high, 8, 7)
    low = totals - high - mid
    split = jnp.stack([high, mid, low], axis=1).astype(BF)
    return jnp.pad(split, ((0, 0), (0, 5), (0, width - totals.shape[1])))


def root_norm(values):
    return values * lax.rsqrt(jnp.mean(values * values, axis=-1, keepdims=True) + 1e-06)


def body(frames, qkv_weight, attn_out_weight, head_weight, back_weight):
    rows = frames.shape[0]
    width = frames.shape[1]
    planes = lax.axis_size(PLANE)
    cols = lax.axis_size(COL)
    block = rows * cols
    far = WIN - block
    full_head = over_time(head_weight, 0)
    full_back = over_time(back_weight, 1)

    own = gathered(frames, COL)
    prev = passed_along(own, BLOCKS, 1)
    prev2 = passed_along(own[block - far :], BLOCKS, 2)
    keys = WIN + block
    normed = root_norm(jnp.concatenate([prev2, prev, own], axis=0).astype(F32)).astype(BF)
    project = jnp.dot(normed, qkv_weight, preferred_element_type=F32).astype(BF)
    query = project[WIN:, :width].reshape(block, HEADS, HEAD_DIM)
    key_part = project[:, width : 2 * width].reshape(keys, HEADS, HEAD_DIM)
    value_part = project[:, 2 * width :].reshape(keys, HEADS, HEAD_DIM)
    first = lax.axis_index(BLOCKS) * block
    query_pos = first + jnp.arange(block, dtype=jnp.int32)
    key_pos = first - WIN + jnp.arange(keys, dtype=jnp.int32)
    scores = jnp.einsum(
        "qhd,khd->hqk", query, key_part, preferred_element_type=F32
    ) / math.sqrt(HEAD_DIM)
    scores = 50.0 * jnp.tanh(scores / 50.0)
    allowed = (
        (key_pos[None, :] <= query_pos[:, None])
        & (key_pos[None, :] > query_pos[:, None] - WIN)
        & (key_pos[None, :] >= 0)
    )
    expo = jnp.where(allowed[None], jnp.exp(scores), 0.0)
    weights = (expo / jnp.sum(expo, axis=-1, keepdims=True)).astype(BF)
    context = jnp.einsum("hqk,khd->qhd", weights, value_part, preferred_element_type=F32)
    context = context.astype(BF).reshape(block, width)
    hidden = (
        own.astype(F32) + jnp.dot(context, attn_out_weight, preferred_element_type=F32)
    ).astype(BF)
    unit = root_norm(hidden.astype(F32)).astype(BF)

    unit = from_own(unit).reshape(cols, rows, width)
    totals = []
    partials = []
    for first_row, last_row in CHUNKS:
        count = last_row - first_row
        piece = unit[:, first_row:last_row].reshape(cols * count, width)
        piece = gathered(piece, PLANE)
        logits = jnp.dot(piece, full_head, preferred_element_type=F32)
        label_probs = jnp.exp(30.0 * jnp.tanh(logits / 30.0)).astype(BF)
        total = jnp.sum(label_probs.astype(F32), axis=-1)
        totals.append(total.reshape(planes, cols * count))
        partial = jnp.dot(label_probs, full_back, preferred_element_type=F32).astype(BF)
        partials.append(partial.reshape(planes, cols * count, width))
    sent = jnp.concatenate(partials + [three_rows(jnp.concatenate(totals, axis=1), width)], axis=1)
    summed = jnp.sum(lax.all_to_all(sent, PLANE, 0, 0).astype(F32), axis=0)
    block_totals = jnp.sum(summed[block : block + 3, :block], axis=0)
    sums = []
    ordered = []
    for first_row, last_row in CHUNKS:
        part = slice(cols * first_row, cols * last_row)
        sums.append(summed[part].astype(BF).reshape(cols, last_row - first_row, width))
        ordered.append(block_totals[part].reshape(cols, last_row - first_row))
    split = three_rows(jnp.concatenate(ordered, axis=1), width)
    sent = jnp.concatenate(sums + [split], axis=1)
    summed = jnp.sum(lax.all_to_all(sent, COL, 0, 0).astype(F32), axis=0)
    owned_totals = jnp.sum(summed[rows : rows + 3, :rows], axis=0)
    back_proj = from_own(summed[:rows]) / owned_totals[:, None]

    own_hidden = lax.dynamic_slice_in_dim(hidden, lax.axis_index(COL) * rows, rows, 0)
    center = back_proj - jnp.mean(back_proj, axis=-1, keepdims=True)
    spread = jnp.mean(center * center, axis=-1, keepdims=True)
    conditioned = (own_hidden.astype(F32) + center * lax.rsqrt(spread + 1e-05)).astype(BF)
    return (conditioned, jnp.log(owned_totals))


def solution(mesh):
    cube = Mesh(mesh.devices.reshape(2, 2, 4, 4, 4), EVERY)
    return jax.shard_map(
        body,
        mesh=cube,
        in_specs=(P(EVERY, None), P(), P(), P(TIME, PLANE + (COL,)), P(PLANE + (COL,), TIME)),
        out_specs=(P(EVERY, None), P(EVERY)),
        check_vma=False,
    )
```

```python
import math

import jax
import jax.numpy as jnp
from jax import lax
from jax.sharding import Mesh, PartitionSpec as P


HEADS = 16
HEAD_DIM = 64
WIN = 128
BF = jnp.bfloat16
F32 = jnp.float32
TIME = ("zl", "c")
PLANE = ("x", "y")
COL = "zh"
BLOCKS = TIME + PLANE
EVERY = BLOCKS + (COL,)


def gathered(block, axes):
    size = lax.axis_size(axes)
    copies = lax.optimization_barrier(jnp.broadcast_to(block[None], (size,) + block.shape))
    parts = lax.all_to_all(copies, axes, 0, 0)
    return parts.reshape((size * block.shape[0],) + block.shape[1:])


def passed_along(block, axes, distance):
    devices = range(lax.axis_size(axes))
    route = [(i, i + distance) for i in devices if i + distance in devices]
    return lax.ppermute(block, axes, route)


def swapped(block, axis):
    return lax.ppermute(block, axis, [(0, 1), (1, 0)])


def over_time(block, axis):
    beside = swapped(block, "c")
    across = swapped(block, "zl")
    corner = swapped(across, "c")
    return jnp.concatenate([block, beside, across, corner], axis=axis)


def from_own(values):
    quarter = values.shape[1] // 4
    q = [values[:, i * quarter : (i + 1) * quarter] for i in range(4)]
    odd = lax.axis_index("c") == 1
    q = [jnp.where(odd, q[i ^ 1], q[i]) for i in range(4)]
    late = lax.axis_index("zl") == 1
    return jnp.concatenate([jnp.where(late, q[i ^ 2], q[i]) for i in range(4)], axis=1)


def turned(block, distance):
    size = lax.axis_size(COL)
    return lax.ppermute(block, COL, [(i, (i + distance) % size) for i in range(size)])


def column_rows(block):
    after = [block, turned(block, -1), turned(block, -2), turned(block, 1)]
    place = lax.axis_index(COL)
    odd = place % 2 == 1
    after = [jnp.where(odd, after[i - 1], after[i]) for i in range(4)]
    late = place >= 2
    return jnp.concatenate([jnp.where(late, after[i - 2], after[i]) for i in range(4)], axis=0)


def column_sum(blocks):
    place = lax.axis_index(COL)
    total = lax.dynamic_index_in_dim(blocks, place, 0, False).astype(F32)
    for distance in (1, -1, 2):
        block = lax.dynamic_index_in_dim(blocks, (place + distance) % 4, 0, False)
        total = total + turned(block, distance).astype(F32)
    return total


def three_rows(totals, width):
    high = lax.reduce_precision(totals, 8, 7)
    mid = lax.reduce_precision(totals - high, 8, 7)
    low = totals - high - mid
    split = jnp.stack([high, mid, low], axis=1).astype(BF)
    return jnp.pad(split, ((0, 0), (0, 5), (0, width - totals.shape[1])))


def root_norm(values):
    return values * lax.rsqrt(jnp.mean(values * values, axis=-1, keepdims=True) + 1e-06)


def body(frames, qkv_weight, attn_out_weight, head_weight, back_weight):
    rows = frames.shape[0]
    width = frames.shape[1]
    planes = lax.axis_size(PLANE)
    cols = lax.axis_size(COL)
    block = rows * cols
    far = WIN - block
    full_head = over_time(head_weight, 0)
    full_back = over_time(back_weight, 1)

    own = column_rows(frames)
    prev = passed_along(own, BLOCKS, 1)
    prev2 = passed_along(own[block - far :], BLOCKS, 2)
    keys = WIN + block
    normed = root_norm(jnp.concatenate([prev2, prev, own], axis=0).astype(F32)).astype(BF)
    project = jnp.dot(normed, qkv_weight, preferred_element_type=F32).astype(BF)
    query = project[WIN:, :width].reshape(block, HEADS, HEAD_DIM)
    key_part = project[:, width : 2 * width].reshape(keys, HEADS, HEAD_DIM)
    value_part = project[:, 2 * width :].reshape(keys, HEADS, HEAD_DIM)
    first = lax.axis_index(BLOCKS) * block
    query_pos = first + jnp.arange(block, dtype=jnp.int32)
    key_pos = first - WIN + jnp.arange(keys, dtype=jnp.int32)
    scores = jnp.einsum(
        "qhd,khd->hqk", query, key_part, preferred_element_type=F32
    ) / math.sqrt(HEAD_DIM)
    scores = 50.0 * jnp.tanh(scores / 50.0)
    allowed = (
        (key_pos[None, :] <= query_pos[:, None])
        & (key_pos[None, :] > query_pos[:, None] - WIN)
        & (key_pos[None, :] >= 0)
    )
    expo = jnp.where(allowed[None], jnp.exp(scores), 0.0)
    weights = (expo / jnp.sum(expo, axis=-1, keepdims=True)).astype(BF)
    context = jnp.einsum("hqk,khd->qhd", weights, value_part, preferred_element_type=F32)
    context = context.astype(BF).reshape(block, width)
    hidden = (
        own.astype(F32) + jnp.dot(context, attn_out_weight, preferred_element_type=F32)
    ).astype(BF)
    unit = root_norm(hidden.astype(F32)).astype(BF)

    every = gathered(from_own(unit), PLANE)
    logits = jnp.dot(every, full_head, preferred_element_type=F32)
    label_probs = jnp.exp(30.0 * jnp.tanh(logits / 30.0)).astype(BF)
    totals = jnp.sum(label_probs.astype(F32), axis=-1)
    partial = jnp.dot(label_probs, full_back, preferred_element_type=F32).astype(BF)
    split = three_rows(totals.reshape(planes, block), width)
    sent = jnp.concatenate([partial.reshape(planes, block, width), split], axis=1)
    summed = jnp.sum(lax.all_to_all(sent, PLANE, 0, 0).astype(F32), axis=0)
    block_totals = jnp.sum(summed[block : block + 3, :block], axis=0)
    split = three_rows(block_totals.reshape(cols, rows), width)
    sent = jnp.concatenate([summed[:block].astype(BF).reshape(cols, rows, width), split], axis=1)
    summed = column_sum(sent)
    owned_totals = jnp.sum(summed[rows : rows + 3, :rows], axis=0)
    back_proj = from_own(summed[:rows]) / owned_totals[:, None]

    own_hidden = lax.dynamic_slice_in_dim(hidden, lax.axis_index(COL) * rows, rows, 0)
    center = back_proj - jnp.mean(back_proj, axis=-1, keepdims=True)
    spread = jnp.mean(center * center, axis=-1, keepdims=True)
    conditioned = (own_hidden.astype(F32) + center * lax.rsqrt(spread + 1e-05)).astype(BF)
    return (conditioned, jnp.log(owned_totals))


def solution(mesh):
    cube = Mesh(mesh.devices.reshape(2, 2, 4, 4, 4), EVERY)
    return jax.shard_map(
        body,
        mesh=cube,
        in_specs=(P(EVERY, None), P(), P(), P(TIME, PLANE + (COL,)), P(PLANE + (COL,), TIME)),
        out_specs=(P(EVERY, None), P(EVERY)),
        check_vma=False,
    )
```

```python
import math

import jax
import jax.numpy as jnp
from jax import lax
from jax.sharding import Mesh, PartitionSpec as P


HEADS = 16
HEAD_DIM = 64
WIN = 128
BF = jnp.bfloat16
F32 = jnp.float32
TIME = ("zl", "c")
PLANE = ("x", "y")
COL = "zh"
BLOCKS = TIME + PLANE
EVERY = BLOCKS + (COL,)


def gathered(block, axes):
    size = lax.axis_size(axes)
    copies = lax.optimization_barrier(jnp.broadcast_to(block[None], (size,) + block.shape))
    parts = lax.all_to_all(copies, axes, 0, 0)
    return parts.reshape((size * block.shape[0],) + block.shape[1:])


def passed_along(block, axes, distance):
    devices = range(lax.axis_size(axes))
    route = [(i, i + distance) for i in devices if i + distance in devices]
    return lax.ppermute(block, axes, route)


def swapped(block, axis):
    return lax.ppermute(block, axis, [(0, 1), (1, 0)])


def over_time(block, axis):
    beside = swapped(block, "c")
    across = swapped(block, "zl")
    corner = swapped(across, "c")
    return jnp.concatenate([block, beside, across, corner], axis=axis)


def from_own(values):
    quarter = values.shape[1] // 4
    q = [values[:, i * quarter : (i + 1) * quarter] for i in range(4)]
    odd = lax.axis_index("c") == 1
    q = [jnp.where(odd, q[i ^ 1], q[i]) for i in range(4)]
    late = lax.axis_index("zl") == 1
    return jnp.concatenate([jnp.where(late, q[i ^ 2], q[i]) for i in range(4)], axis=1)


def turned(block, distance):
    size = lax.axis_size(COL)
    return lax.ppermute(block, COL, [(i, (i + distance) % size) for i in range(size)])


def column_rows(block):
    after = [block, turned(block, -1), turned(block, -2), turned(block, 1)]
    place = lax.axis_index(COL)
    odd = place % 2 == 1
    after = [jnp.where(odd, after[i - 1], after[i]) for i in range(4)]
    late = place >= 2
    return jnp.concatenate([jnp.where(late, after[i - 2], after[i]) for i in range(4)], axis=0)


def own_rows_first(block):
    count = block.shape[0] // 4
    q = [block[i * count : (i + 1) * count] for i in range(4)]
    place = lax.axis_index(COL)
    odd = place % 2 == 1
    q = [jnp.where(odd, q[(i + 1) % 4], q[i]) for i in range(4)]
    late = place >= 2
    return jnp.concatenate([jnp.where(late, q[i - 2], q[i]) for i in range(4)], axis=0)


def column_sum(blocks):
    total = blocks[0].astype(F32)
    for distance in (1, 3, 2):
        total = total + turned(blocks[distance], distance).astype(F32)
    return total


def three_rows(totals, width):
    high = lax.reduce_precision(totals, 8, 7)
    mid = lax.reduce_precision(totals - high, 8, 7)
    low = totals - high - mid
    split = jnp.stack([high, mid, low], axis=1).astype(BF)
    return jnp.pad(split, ((0, 0), (0, 5), (0, width - totals.shape[1])))


def root_norm(values):
    return values * lax.rsqrt(jnp.mean(values * values, axis=-1, keepdims=True) + 1e-06)


def body(frames, qkv_weight, attn_out_weight, head_weight, back_weight):
    rows = frames.shape[0]
    width = frames.shape[1]
    planes = lax.axis_size(PLANE)
    cols = lax.axis_size(COL)
    block = rows * cols
    far = WIN - block
    full_head = over_time(head_weight, 0)
    full_back = over_time(back_weight, 1)

    own = column_rows(frames)
    prev = passed_along(own, BLOCKS, 1)
    prev2 = passed_along(own[block - far :], BLOCKS, 2)
    keys = WIN + block
    normed = root_norm(jnp.concatenate([prev2, prev, own], axis=0).astype(F32)).astype(BF)
    project = jnp.dot(normed, qkv_weight, preferred_element_type=F32).astype(BF)
    query = project[WIN:, :width].reshape(block, HEADS, HEAD_DIM)
    key_part = project[:, width : 2 * width].reshape(keys, HEADS, HEAD_DIM)
    value_part = project[:, 2 * width :].reshape(keys, HEADS, HEAD_DIM)
    first = lax.axis_index(BLOCKS) * block
    query_pos = first + jnp.arange(block, dtype=jnp.int32)
    key_pos = first - WIN + jnp.arange(keys, dtype=jnp.int32)
    scores = jnp.einsum(
        "qhd,khd->hqk", query, key_part, preferred_element_type=F32
    ) / math.sqrt(HEAD_DIM)
    scores = 50.0 * jnp.tanh(scores / 50.0)
    allowed = (
        (key_pos[None, :] <= query_pos[:, None])
        & (key_pos[None, :] > query_pos[:, None] - WIN)
        & (key_pos[None, :] >= 0)
    )
    expo = jnp.where(allowed[None], jnp.exp(scores), 0.0)
    weights = (expo / jnp.sum(expo, axis=-1, keepdims=True)).astype(BF)
    context = jnp.einsum("hqk,khd->qhd", weights, value_part, preferred_element_type=F32)
    context = context.astype(BF).reshape(block, width)
    hidden = (
        own.astype(F32) + jnp.dot(context, attn_out_weight, preferred_element_type=F32)
    ).astype(BF)
    hidden = own_rows_first(hidden)
    unit = root_norm(hidden.astype(F32)).astype(BF)

    every = gathered(from_own(unit), PLANE)
    logits = jnp.dot(every, full_head, preferred_element_type=F32)
    label_probs = jnp.exp(30.0 * jnp.tanh(logits / 30.0)).astype(BF)
    totals = jnp.sum(label_probs.astype(F32), axis=-1)
    partial = jnp.dot(label_probs, full_back, preferred_element_type=F32).astype(BF)
    split = three_rows(totals.reshape(planes, block), width)
    sent = jnp.concatenate([partial.reshape(planes, block, width), split], axis=1)
    summed = jnp.sum(lax.all_to_all(sent, PLANE, 0, 0).astype(F32), axis=0)
    block_totals = jnp.sum(summed[block : block + 3, :block], axis=0)
    split = three_rows(block_totals.reshape(cols, rows), width)
    sent = jnp.concatenate([summed[:block].astype(BF).reshape(cols, rows, width), split], axis=1)
    summed = column_sum(sent)
    owned_totals = jnp.sum(summed[rows : rows + 3, :rows], axis=0)
    back_proj = from_own(summed[:rows]) / owned_totals[:, None]

    center = back_proj - jnp.mean(back_proj, axis=-1, keepdims=True)
    spread = jnp.mean(center * center, axis=-1, keepdims=True)
    conditioned = (hidden[:rows].astype(F32) + center * lax.rsqrt(spread + 1e-05)).astype(BF)
    return (conditioned, jnp.log(owned_totals))


def solution(mesh):
    cube = Mesh(mesh.devices.reshape(2, 2, 4, 4, 4), EVERY)
    return jax.shard_map(
        body,
        mesh=cube,
        in_specs=(P(EVERY, None), P(), P(), P(TIME, PLANE + (COL,)), P(PLANE + (COL,), TIME)),
        out_specs=(P(EVERY, None), P(EVERY)),
        check_vma=False,
    )
```

```python
import math

import jax
import jax.numpy as jnp
from jax import lax
from jax.experimental import pallas as pl
from jax.experimental.pallas import tpu as pltpu
from jax.sharding import Mesh, PartitionSpec as P


HEADS = 16
HEAD_DIM = 64
WIN = 128
BF = jnp.bfloat16
F32 = jnp.float32
TIME = ("zl", "c")
PLANE = ("x", "y")
COL = "zh"
BLOCKS = TIME + PLANE
EVERY = BLOCKS + (COL,)


def gathered(block, axes):
    size = lax.axis_size(axes)
    copies = lax.optimization_barrier(jnp.broadcast_to(block[None], (size,) + block.shape))
    parts = lax.all_to_all(copies, axes, 0, 0)
    return parts.reshape((size * block.shape[0],) + block.shape[1:])


def passed_along(block, axes, distance):
    devices = range(lax.axis_size(axes))
    route = [(i, i + distance) for i in devices if i + distance in devices]
    return lax.ppermute(block, axes, route)


def swapped(block, axis):
    return lax.ppermute(block, axis, [(0, 1), (1, 0)])


def over_time(block):
    beside = swapped(block, "c")
    across = swapped(block, "zl")
    corner = swapped(across, "c")
    return block, beside, across, corner


def from_own(values):
    quarter = values.shape[1] // 4
    q = [values[:, i * quarter : (i + 1) * quarter] for i in range(4)]
    odd = lax.axis_index("c") == 1
    q = [jnp.where(odd, q[i ^ 1], q[i]) for i in range(4)]
    late = lax.axis_index("zl") == 1
    return jnp.concatenate([jnp.where(late, q[i ^ 2], q[i]) for i in range(4)], axis=1)


def turned(block, distance):
    size = lax.axis_size(COL)
    return lax.ppermute(block, COL, [(i, (i + distance) % size) for i in range(size)])


def column_rows(block):
    after = [block, turned(block, -1), turned(block, -2), turned(block, 1)]
    place = lax.axis_index(COL)
    odd = place % 2 == 1
    after = [jnp.where(odd, after[i - 1], after[i]) for i in range(4)]
    late = place >= 2
    return jnp.concatenate([jnp.where(late, after[i - 2], after[i]) for i in range(4)], axis=0)


def own_rows_first(block):
    count = block.shape[0] // 4
    q = [block[i * count : (i + 1) * count] for i in range(4)]
    place = lax.axis_index(COL)
    odd = place % 2 == 1
    q = [jnp.where(odd, q[(i + 1) % 4], q[i]) for i in range(4)]
    late = place >= 2
    return jnp.concatenate([jnp.where(late, q[i - 2], q[i]) for i in range(4)], axis=0)


def column_sum(blocks):
    total = blocks[0].astype(F32)
    for distance in (1, 3, 2):
        total = total + turned(blocks[distance], distance).astype(F32)
    return total


def three_rows(totals, width):
    high = lax.reduce_precision(totals, 8, 7)
    mid = lax.reduce_precision(totals - high, 8, 7)
    low = totals - high - mid
    split = jnp.stack([high, mid, low], axis=1).astype(BF)
    return jnp.pad(split, ((0, 0), (0, 5), (0, width - totals.shape[1])))


def root_norm(values):
    return values * lax.rsqrt(jnp.mean(values * values, axis=-1, keepdims=True) + 1e-06)


STEPS = 4
PARTS = 4


def label_kernel(unit_ref, h0, h1, h2, h3, b0, b1, b2, b3, out_ref, head, back, total, sums, sems):
    step = pl.program_id(0)
    labels = head.shape[1] // PARTS
    count = out_ref.shape[0]
    block = unit_ref.shape[0] // count
    narrow = back.shape[1] // PARTS
    pieces = ((h0, h1, h2, h3), (b0, b1, b2, b3))

    def copies(kind, part):
        span = slice(part * labels, (part + 1) * labels)
        for q in range(PARTS):
            if kind == 0:
                source = pieces[0][q].at[:, span]
                target = head.at[q * 256 : (q + 1) * 256, span]
            else:
                source = pieces[1][q].at[span, :]
                target = back.at[span, q * narrow : (q + 1) * narrow]
            yield pltpu.make_async_copy(source, target, sems.at[kind, part, q])

    @pl.when(step == 0)
    def _():
        for part in range(PARTS):
            for kind in range(2):
                for copy in copies(kind, part):
                    copy.start()

    def arrive(kind, part):
        @pl.when(step == 0)
        def _():
            for copy in copies(kind, part):
                copy.wait()

    def logits(part):
        arrive(0, part)
        span = slice(part * labels, (part + 1) * labels)
        return jnp.dot(unit_ref[...], head[:, span], preferred_element_type=F32)

    ahead = logits(0)
    lanes = None
    for part in range(PARTS):
        now = ahead
        if part + 1 < PARTS:
            ahead = logits(part + 1)
        arrive(1, part)
        probs = jnp.exp(30.0 * jnp.tanh(now * (1.0 / 30.0))).astype(BF)
        wide = probs.astype(F32)
        for k in range(labels // 128):
            column = wide[:, k * 128 : (k + 1) * 128]
            lanes = column if lanes is None else lanes + column
        span = slice(part * labels, (part + 1) * labels)
        value = jnp.dot(probs, back[span, :], preferred_element_type=F32)
        if part == 0:
            total[...] = value
        else:
            total[...] += value
    sums[0 : count * block, :] = lanes
    sums[count * block :, :] = jnp.zeros((sums.shape[0] - count * block, 128), F32)
    row = lax.broadcasted_iota(jnp.int32, (8, 128), 0)
    for s in range(count):
        for j in range(total.shape[1] // 128):
            tile = total[s * block : (s + 1) * block, j * 128 : (j + 1) * 128]
            out_ref[s, j * block : (j + 1) * block, :] = tile.astype(BF)
        flat = jnp.sum(sums[s * block : s * block + 128, :].T, axis=0, keepdims=True)
        high = flat.astype(BF).astype(F32)
        mid = (flat - high).astype(BF).astype(F32)
        low = flat - high - mid
        split = jnp.where(row == 0, high, jnp.where(row == 1, mid, jnp.where(row == 2, low, 0.0)))
        out_ref[s, 8 * block :, :] = split.astype(BF)


def label_sums(unit, head_parts, back_parts):
    frames, width = unit.shape
    labels = head_parts[0].shape[1]
    slots = 16
    block = frames // slots
    count = slots // STEPS
    rows = 8 * block + 8
    return pl.pallas_call(
        label_kernel,
        grid=(STEPS,),
        in_specs=[pl.BlockSpec((count * block, width), lambda i: (i, 0))]
        + [pl.BlockSpec(memory_space=pl.ANY)] * 8,
        out_specs=pl.BlockSpec((count, rows, 128), lambda i: (i, 0, 0)),
        out_shape=jax.ShapeDtypeStruct((slots, rows, 128), BF),
        scratch_shapes=[
            pltpu.VMEM((width, labels), BF),
            pltpu.VMEM((labels, width), BF),
            pltpu.VMEM((count * block, width), F32),
            pltpu.VMEM((count * block + 32, 128), F32),
            pltpu.SemaphoreType.DMA((2, PARTS, 4)),
        ],
        compiler_params=pltpu.CompilerParams(vmem_limit_bytes=40 * 2**20),
        cost_estimate=pl.CostEstimate(
            flops=4 * frames * width * labels, bytes_accessed=16 * 2**20, transcendentals=2 * frames * labels
        ),
    )(unit, *head_parts, *back_parts)


def body(frames, qkv_weight, attn_out_weight, head_weight, back_weight):
    rows = frames.shape[0]
    width = frames.shape[1]
    cols = lax.axis_size(COL)
    block = rows * cols
    far = WIN - block
    head_parts = over_time(head_weight)
    back_parts = over_time(back_weight)

    own = column_rows(frames)
    prev = passed_along(own, BLOCKS, 1)
    prev2 = passed_along(own[block - far :], BLOCKS, 2)
    keys = WIN + block
    normed = root_norm(jnp.concatenate([prev2, prev, own], axis=0).astype(F32)).astype(BF)
    project = jnp.dot(normed, qkv_weight, preferred_element_type=F32).astype(BF)
    query = project[WIN:, :width].reshape(block, HEADS, HEAD_DIM)
    key_part = project[:, width : 2 * width].reshape(keys, HEADS, HEAD_DIM)
    value_part = project[:, 2 * width :].reshape(keys, HEADS, HEAD_DIM)
    first = lax.axis_index(BLOCKS) * block
    query_pos = first + jnp.arange(block, dtype=jnp.int32)
    key_pos = first - WIN + jnp.arange(keys, dtype=jnp.int32)
    scores = jnp.einsum(
        "qhd,khd->hqk", query, key_part, preferred_element_type=F32
    ) / math.sqrt(HEAD_DIM)
    scores = 50.0 * jnp.tanh(scores / 50.0)
    allowed = (
        (key_pos[None, :] <= query_pos[:, None])
        & (key_pos[None, :] > query_pos[:, None] - WIN)
        & (key_pos[None, :] >= 0)
    )
    expo = jnp.where(allowed[None], jnp.exp(scores), 0.0)
    weights = (expo / jnp.sum(expo, axis=-1, keepdims=True)).astype(BF)
    context = jnp.einsum("hqk,khd->qhd", weights, value_part, preferred_element_type=F32)
    context = context.astype(BF).reshape(block, width)
    hidden = (
        own.astype(F32) + jnp.dot(context, attn_out_weight, preferred_element_type=F32)
    ).astype(BF)
    hidden = own_rows_first(hidden)
    unit = root_norm(hidden.astype(F32)).astype(BF)

    every = gathered(from_own(unit), PLANE)
    sent = label_sums(every, head_parts, back_parts)
    summed = jnp.sum(lax.all_to_all(sent, PLANE, 0, 0).astype(F32), axis=0)
    block_totals = jnp.sum(summed[8 * block : 8 * block + 3, :block], axis=0)
    split = three_rows(block_totals.reshape(cols, rows), 128)
    parts = summed[: 8 * block].astype(BF).reshape(8, cols, rows, 128).transpose(1, 0, 2, 3)
    sent = jnp.concatenate([parts.reshape(cols, 8 * rows, 128), split], axis=1)
    summed = column_sum(sent)
    owned_totals = jnp.sum(summed[8 * rows : 8 * rows + 3, :rows], axis=0)
    back_proj = summed[: 8 * rows].reshape(8, rows, 128).transpose(1, 0, 2).reshape(rows, width)
    back_proj = from_own(back_proj) / owned_totals[:, None]

    center = back_proj - jnp.mean(back_proj, axis=-1, keepdims=True)
    spread = jnp.mean(center * center, axis=-1, keepdims=True)
    conditioned = (hidden[:rows].astype(F32) + center * lax.rsqrt(spread + 1e-05)).astype(BF)
    return (conditioned, jnp.log(owned_totals))


def solution(mesh):
    cube = Mesh(mesh.devices.reshape(2, 2, 4, 4, 4), EVERY)
    return jax.shard_map(
        body,
        mesh=cube,
        in_specs=(P(EVERY, None), P(), P(), P(TIME, PLANE + (COL,)), P(PLANE + (COL,), TIME)),
        out_specs=(P(EVERY, None), P(EVERY)),
        check_vma=False,
    )
```

```python
import math

import jax
import jax.numpy as jnp
from jax import lax
from jax.experimental import pallas as pl
from jax.experimental.pallas import tpu as pltpu
from jax.sharding import Mesh, PartitionSpec as P


HEADS = 16
HEAD_DIM = 64
WIN = 128
BF = jnp.bfloat16
F32 = jnp.float32
TIME = ("zl", "c")
PLANE = ("x", "y")
COL = "zh"
BLOCKS = TIME + PLANE
EVERY = BLOCKS + (COL,)


def gathered(block, axes):
    size = lax.axis_size(axes)
    copies = lax.optimization_barrier(jnp.broadcast_to(block[None], (size,) + block.shape))
    parts = lax.all_to_all(copies, axes, 0, 0)
    return parts.reshape((size * block.shape[0],) + block.shape[1:])


def passed_along(block, axes, distance):
    devices = range(lax.axis_size(axes))
    route = [(i, i + distance) for i in devices if i + distance in devices]
    return lax.ppermute(block, axes, route)


def swapped(block, axis):
    return lax.ppermute(block, axis, [(0, 1), (1, 0)])


def over_time(block):
    beside = swapped(block, "c")
    across = swapped(block, "zl")
    corner = swapped(across, "c")
    return block, beside, across, corner


def from_own(values):
    quarter = values.shape[1] // 4
    q = [values[:, i * quarter : (i + 1) * quarter] for i in range(4)]
    odd = lax.axis_index("c") == 1
    q = [jnp.where(odd, q[i ^ 1], q[i]) for i in range(4)]
    late = lax.axis_index("zl") == 1
    return jnp.concatenate([jnp.where(late, q[i ^ 2], q[i]) for i in range(4)], axis=1)


def turned(block, distance):
    size = lax.axis_size(COL)
    return lax.ppermute(block, COL, [(i, (i + distance) % size) for i in range(size)])


def column_rows(block):
    after = [block, turned(block, -1), turned(block, -2), turned(block, 1)]
    place = lax.axis_index(COL)
    odd = place % 2 == 1
    after = [jnp.where(odd, after[i - 1], after[i]) for i in range(4)]
    late = place >= 2
    return jnp.concatenate([jnp.where(late, after[i - 2], after[i]) for i in range(4)], axis=0)


def own_rows_first(block):
    count = block.shape[0] // 4
    q = [block[i * count : (i + 1) * count] for i in range(4)]
    place = lax.axis_index(COL)
    odd = place % 2 == 1
    q = [jnp.where(odd, q[(i + 1) % 4], q[i]) for i in range(4)]
    late = place >= 2
    return jnp.concatenate([jnp.where(late, q[i - 2], q[i]) for i in range(4)], axis=0)


def column_sum(blocks):
    total = blocks[0].astype(F32)
    for distance in (1, 3, 2):
        total = total + turned(blocks[distance], distance).astype(F32)
    return total


def three_rows(totals, width):
    high = lax.reduce_precision(totals, 8, 7)
    mid = lax.reduce_precision(totals - high, 8, 7)
    low = totals - high - mid
    split = jnp.stack([high, mid, low], axis=1).astype(BF)
    return jnp.pad(split, ((0, 0), (0, 5), (0, width - totals.shape[1])))


def root_norm(values):
    return values * lax.rsqrt(jnp.mean(values * values, axis=-1, keepdims=True) + 1e-06)


STEPS = 4
PARTS = 4


def label_kernel(unit_ref, h0, h1, h2, h3, b0, b1, b2, b3, out_ref, head, back, total, sums, sems):
    step = pl.program_id(0)
    labels = head.shape[1] // PARTS
    count = out_ref.shape[0]
    block = unit_ref.shape[0] // count
    narrow = back.shape[1] // PARTS
    pieces = ((h0, h1, h2, h3), (b0, b1, b2, b3))

    def copies(kind, part):
        span = slice(part * labels, (part + 1) * labels)
        for q in range(PARTS):
            if kind == 0:
                source = pieces[0][q].at[:, span]
                target = head.at[q * 256 : (q + 1) * 256, span]
            else:
                source = pieces[1][q].at[span, :]
                target = back.at[span, q * narrow : (q + 1) * narrow]
            yield pltpu.make_async_copy(source, target, sems.at[kind, part, q])

    @pl.when(step == 0)
    def _():
        for part in range(PARTS):
            for kind in range(2):
                for copy in copies(kind, part):
                    copy.start()

    def arrive(kind, part):
        @pl.when(step == 0)
        def _():
            for copy in copies(kind, part):
                copy.wait()

    def logits(part):
        arrive(0, part)
        span = slice(part * labels, (part + 1) * labels)
        return jnp.dot(unit_ref[...], head[:, span], preferred_element_type=F32)

    ahead = logits(0)
    lanes = None
    for part in range(PARTS):
        now = ahead
        if part + 1 < PARTS:
            ahead = logits(part + 1)
        arrive(1, part)
        probs = jnp.exp(30.0 * jnp.tanh(now * (1.0 / 30.0))).astype(BF)
        wide = probs.astype(F32)
        for k in range(labels // 128):
            column = wide[:, k * 128 : (k + 1) * 128]
            lanes = column if lanes is None else lanes + column
        span = slice(part * labels, (part + 1) * labels)
        value = jnp.dot(probs, back[span, :], preferred_element_type=F32)
        if part == 0:
            total[...] = value
        else:
            total[...] += value
    sums[0 : count * block, :] = lanes
    sums[count * block :, :] = jnp.zeros((sums.shape[0] - count * block, 128), F32)
    row = lax.broadcasted_iota(jnp.int32, (8, 128), 0)
    for s in range(count):
        for j in range(total.shape[1] // 128):
            tile = total[s * block : (s + 1) * block, j * 128 : (j + 1) * 128]
            out_ref[s, j * block : (j + 1) * block, :] = tile.astype(BF)
        flat = jnp.sum(sums[s * block : s * block + 128, :].T, axis=0, keepdims=True)
        high = flat.astype(BF).astype(F32)
        mid = (flat - high).astype(BF).astype(F32)
        low = flat - high - mid
        split = jnp.where(row == 0, high, jnp.where(row == 1, mid, jnp.where(row == 2, low, 0.0)))
        out_ref[s, 8 * block :, :] = split.astype(BF)


def label_sums(unit, head_parts, back_parts):
    frames, width = unit.shape
    labels = head_parts[0].shape[1]
    slots = 16
    block = frames // slots
    count = slots // STEPS
    rows = 8 * block + 8
    return pl.pallas_call(
        label_kernel,
        grid=(STEPS,),
        in_specs=[pl.BlockSpec((count * block, width), lambda i: (i, 0))]
        + [pl.BlockSpec(memory_space=pltpu.HBM)] * 8,
        out_specs=pl.BlockSpec((count, rows, 128), lambda i: (i, 0, 0)),
        out_shape=jax.ShapeDtypeStruct((slots, rows, 128), BF),
        scratch_shapes=[
            pltpu.VMEM((width, labels), BF),
            pltpu.VMEM((labels, width), BF),
            pltpu.VMEM((count * block, width), F32),
            pltpu.VMEM((count * block + 32, 128), F32),
            pltpu.SemaphoreType.DMA((2, PARTS, 4)),
        ],
        compiler_params=pltpu.CompilerParams(vmem_limit_bytes=20 * 2**20),
        cost_estimate=pl.CostEstimate(
            flops=4 * frames * width * labels, bytes_accessed=16 * 2**20, transcendentals=2 * frames * labels
        ),
    )(unit, *[pltpu.with_memory_space_constraint(p, pltpu.HBM) for p in (*head_parts, *back_parts)])


def body(frames, qkv_weight, attn_out_weight, head_weight, back_weight):
    rows = frames.shape[0]
    width = frames.shape[1]
    cols = lax.axis_size(COL)
    block = rows * cols
    far = WIN - block
    head_parts = over_time(head_weight)
    back_parts = over_time(back_weight)

    own = column_rows(frames)
    prev = passed_along(own, BLOCKS, 1)
    prev2 = passed_along(own[block - far :], BLOCKS, 2)
    keys = WIN + block
    normed = root_norm(jnp.concatenate([prev2, prev, own], axis=0).astype(F32)).astype(BF)
    project = jnp.dot(normed, qkv_weight, preferred_element_type=F32).astype(BF)
    query = project[WIN:, :width].reshape(block, HEADS, HEAD_DIM)
    key_part = project[:, width : 2 * width].reshape(keys, HEADS, HEAD_DIM)
    value_part = project[:, 2 * width :].reshape(keys, HEADS, HEAD_DIM)
    first = lax.axis_index(BLOCKS) * block
    query_pos = first + jnp.arange(block, dtype=jnp.int32)
    key_pos = first - WIN + jnp.arange(keys, dtype=jnp.int32)
    scores = jnp.einsum(
        "qhd,khd->hqk", query, key_part, preferred_element_type=F32
    ) / math.sqrt(HEAD_DIM)
    scores = 50.0 * jnp.tanh(scores / 50.0)
    allowed = (
        (key_pos[None, :] <= query_pos[:, None])
        & (key_pos[None, :] > query_pos[:, None] - WIN)
        & (key_pos[None, :] >= 0)
    )
    expo = jnp.where(allowed[None], jnp.exp(scores), 0.0)
    weights = (expo / jnp.sum(expo, axis=-1, keepdims=True)).astype(BF)
    context = jnp.einsum("hqk,khd->qhd", weights, value_part, preferred_element_type=F32)
    context = context.astype(BF).reshape(block, width)
    hidden = (
        own.astype(F32) + jnp.dot(context, attn_out_weight, preferred_element_type=F32)
    ).astype(BF)
    hidden = own_rows_first(hidden)
    unit = root_norm(hidden.astype(F32)).astype(BF)

    every = gathered(from_own(unit), PLANE)
    sent = label_sums(every, head_parts, back_parts)
    summed = jnp.sum(lax.all_to_all(sent, PLANE, 0, 0).astype(F32), axis=0)
    block_totals = jnp.sum(summed[8 * block : 8 * block + 3, :block], axis=0)
    split = three_rows(block_totals.reshape(cols, rows), 128)
    parts = summed[: 8 * block].astype(BF).reshape(8, cols, rows, 128).transpose(1, 0, 2, 3)
    sent = jnp.concatenate([parts.reshape(cols, 8 * rows, 128), split], axis=1)
    summed = column_sum(sent)
    owned_totals = jnp.sum(summed[8 * rows : 8 * rows + 3, :rows], axis=0)
    back_proj = summed[: 8 * rows].reshape(8, rows, 128).transpose(1, 0, 2).reshape(rows, width)
    back_proj = from_own(back_proj) / owned_totals[:, None]

    center = back_proj - jnp.mean(back_proj, axis=-1, keepdims=True)
    spread = jnp.mean(center * center, axis=-1, keepdims=True)
    conditioned = (hidden[:rows].astype(F32) + center * lax.rsqrt(spread + 1e-05)).astype(BF)
    return (conditioned, jnp.log(owned_totals))


def solution(mesh):
    cube = Mesh(mesh.devices.reshape(2, 2, 4, 4, 4), EVERY)
    return jax.shard_map(
        body,
        mesh=cube,
        in_specs=(P(EVERY, None), P(), P(), P(TIME, PLANE + (COL,)), P(PLANE + (COL,), TIME)),
        out_specs=(P(EVERY, None), P(EVERY)),
        check_vma=False,
    )
```

```python
import math

import jax
import jax.numpy as jnp
from jax import lax
from jax.experimental import pallas as pl
from jax.experimental.pallas import tpu as pltpu
from jax.sharding import Mesh, PartitionSpec as P


HEADS = 16
HEAD_DIM = 64
WIN = 128
BF = jnp.bfloat16
F32 = jnp.float32
TIME = ("zl", "c")
PLANE = ("x", "y")
COL = "zh"
BLOCKS = TIME + PLANE
EVERY = BLOCKS + (COL,)


def gathered(block, axes):
    size = lax.axis_size(axes)
    copies = lax.optimization_barrier(jnp.broadcast_to(block[None], (size,) + block.shape))
    parts = lax.all_to_all(copies, axes, 0, 0)
    return parts.reshape((size * block.shape[0],) + block.shape[1:])


def passed_along(block, axes, distance):
    devices = range(lax.axis_size(axes))
    route = [(i, i + distance) for i in devices if i + distance in devices]
    return lax.ppermute(block, axes, route)


def swapped(block, axis):
    return lax.ppermute(block, axis, [(0, 1), (1, 0)])


def over_time(block):
    beside = swapped(block, "c")
    across = swapped(block, "zl")
    corner = swapped(across, "c")
    return block, beside, across, corner


def from_own(values):
    quarter = values.shape[1] // 4
    q = [values[:, i * quarter : (i + 1) * quarter] for i in range(4)]
    odd = lax.axis_index("c") == 1
    q = [jnp.where(odd, q[i ^ 1], q[i]) for i in range(4)]
    late = lax.axis_index("zl") == 1
    return jnp.concatenate([jnp.where(late, q[i ^ 2], q[i]) for i in range(4)], axis=1)


def turned(block, distance):
    size = lax.axis_size(COL)
    return lax.ppermute(block, COL, [(i, (i + distance) % size) for i in range(size)])


def column_rows(block):
    after = [block, turned(block, -1), turned(block, -2), turned(block, 1)]
    place = lax.axis_index(COL)
    odd = place % 2 == 1
    after = [jnp.where(odd, after[i - 1], after[i]) for i in range(4)]
    late = place >= 2
    return jnp.concatenate([jnp.where(late, after[i - 2], after[i]) for i in range(4)], axis=0)


def own_rows_first(block):
    count = block.shape[0] // 4
    q = [block[i * count : (i + 1) * count] for i in range(4)]
    place = lax.axis_index(COL)
    odd = place % 2 == 1
    q = [jnp.where(odd, q[(i + 1) % 4], q[i]) for i in range(4)]
    late = place >= 2
    return jnp.concatenate([jnp.where(late, q[i - 2], q[i]) for i in range(4)], axis=0)


def column_sum(blocks):
    total = blocks[0].astype(F32)
    for distance in (1, 3, 2):
        block = turned(blocks[distance], distance)
        total = total + block.astype(F32)
    return total


def three_rows(totals, width):
    high = lax.reduce_precision(totals, 8, 7)
    mid = lax.reduce_precision(totals - high, 8, 7)
    low = totals - high - mid
    split = jnp.stack([high, mid, low], axis=1).astype(BF)
    return jnp.pad(split, ((0, 0), (0, 5), (0, width - totals.shape[1])))


def root_norm(values):
    return values * lax.rsqrt(jnp.mean(values * values, axis=-1, keepdims=True) + 1e-06)


STEPS = 4
PARTS = 4


def label_kernel(unit_ref, h0, h1, h2, h3, b0, b1, b2, b3, out_ref, head, back, total, sums, sems):
    step = pl.program_id(0)
    labels = head.shape[1] // PARTS
    count = out_ref.shape[0]
    block = unit_ref.shape[0] // count
    narrow = back.shape[1] // PARTS
    pieces = ((h0, h1, h2, h3), (b0, b1, b2, b3))

    def copies(kind, part):
        span = slice(part * labels, (part + 1) * labels)
        for q in range(PARTS):
            if kind == 0:
                source = pieces[0][q].at[:, span]
                target = head.at[q * 256 : (q + 1) * 256, span]
            else:
                source = pieces[1][q].at[span, :]
                target = back.at[span, q * narrow : (q + 1) * narrow]
            yield pltpu.make_async_copy(source, target, sems.at[kind, part, q])

    @pl.when(step == 0)
    def _():
        for part in range(PARTS):
            for kind in range(2):
                for copy in copies(kind, part):
                    copy.start()

    def arrive(kind, part):
        @pl.when(step == 0)
        def _():
            for copy in copies(kind, part):
                copy.wait()

    def logits(part):
        arrive(0, part)
        span = slice(part * labels, (part + 1) * labels)
        return jnp.dot(unit_ref[...], head[:, span], preferred_element_type=F32)

    ahead = logits(0)
    lanes = None
    for part in range(PARTS):
        now = ahead
        if part + 1 < PARTS:
            ahead = logits(part + 1)
        arrive(1, part)
        probs = jnp.exp(30.0 * jnp.tanh(now * (1.0 / 30.0))).astype(BF)
        wide = probs.astype(F32)
        for k in range(labels // 128):
            column = wide[:, k * 128 : (k + 1) * 128]
            lanes = column if lanes is None else lanes + column
        span = slice(part * labels, (part + 1) * labels)
        value = jnp.dot(probs, back[span, :], preferred_element_type=F32)
        if part == 0:
            total[...] = value
        else:
            total[...] += value
    sums[0 : count * block, :] = lanes
    sums[count * block :, :] = jnp.zeros((sums.shape[0] - count * block, 128), F32)
    row = lax.broadcasted_iota(jnp.int32, (8, 128), 0)
    for s in range(count):
        for j in range(total.shape[1] // 128):
            tile = total[s * block : (s + 1) * block, j * 128 : (j + 1) * 128]
            out_ref[s, j * block : (j + 1) * block, :] = tile.astype(BF)
        flat = jnp.sum(sums[s * block : s * block + 128, :].T, axis=0, keepdims=True)
        high = flat.astype(BF).astype(F32)
        mid = (flat - high).astype(BF).astype(F32)
        low = flat - high - mid
        split = jnp.where(row == 0, high, jnp.where(row == 1, mid, jnp.where(row == 2, low, 0.0)))
        out_ref[s, 8 * block :, :] = split.astype(BF)


def label_sums(unit, head_parts, back_parts):
    frames, width = unit.shape
    labels = head_parts[0].shape[1]
    slots = 16
    block = frames // slots
    count = slots // STEPS
    rows = 8 * block + 8
    return pl.pallas_call(
        label_kernel,
        grid=(STEPS,),
        in_specs=[pl.BlockSpec((count * block, width), lambda i: (i, 0))]
        + [pl.BlockSpec(memory_space=pltpu.HBM)] * 8,
        out_specs=pl.BlockSpec((count, rows, 128), lambda i: (i, 0, 0)),
        out_shape=jax.ShapeDtypeStruct((slots, rows, 128), BF),
        scratch_shapes=[
            pltpu.VMEM((width, labels), BF),
            pltpu.VMEM((labels, width), BF),
            pltpu.VMEM((count * block, width), F32),
            pltpu.VMEM((count * block + 32, 128), F32),
            pltpu.SemaphoreType.DMA((2, PARTS, 4)),
        ],
        compiler_params=pltpu.CompilerParams(vmem_limit_bytes=20 * 2**20),
        cost_estimate=pl.CostEstimate(
            flops=4 * frames * width * labels, bytes_accessed=16 * 2**20, transcendentals=2 * frames * labels
        ),
    )(unit, *[pltpu.with_memory_space_constraint(p, pltpu.HBM) for p in (*head_parts, *back_parts)])


def attention_kernel(first_ref, far_ref, near_ref, own_ref, qkv_ref, merge_ref, out_ref, normed, query, key, value, context,
                     weight, merge, sems):
    block, width = own_ref.shape
    wide = weight.shape[2]
    many = weight.shape[0]
    copies = [
        pltpu.make_async_copy(qkv_ref.at[:, i * wide : (i + 1) * wide], weight.at[i], sems.at[i])
        for i in range(many)
    ] + [pltpu.make_async_copy(merge_ref, merge, sems.at[many])]
    for copy in copies:
        copy.start()
    past = far_ref.shape[0] + near_ref.shape[0]
    keys = past + block
    row = 0
    for ref in (far_ref, near_ref, own_ref):
        normed[row : row + ref.shape[0], :] = root_norm(ref[...].astype(F32)).astype(BF)
        row += ref.shape[0]
    for i in range(many):
        copies[i].wait()
        part, start = divmod(i * wide, width)
        ref = (query, key, value)[part]
        span = slice(start, start + wide)
        lowest = past if part == 0 else 0
        product = jnp.dot(normed[lowest:keys, :], weight[i], preferred_element_type=F32)
        ref[0 : keys - lowest, span] = product.astype(BF)
        if part:
            ref[keys:, span] = jnp.zeros((ref.shape[0] - keys, wide), BF)
    padded = key.shape[0]
    r = lax.broadcasted_iota(jnp.int32, (block, padded), 0)
    j = lax.broadcasted_iota(jnp.int32, (block, padded), 1)
    allowed = (j <= r + past) & (j > r + past - WIN) & (j < keys) & (first_ref[0] - past + j >= 0)
    lane = lax.broadcasted_iota(jnp.int32, (block, 128), 1)
    for pair in range(width // 128):
        span = slice(pair * 128, (pair + 1) * 128)
        both = query[:, span].astype(F32)
        parts = []
        for side in range(2):
            mine = (lane >= HEAD_DIM) == (side == 1)
            one = jnp.where(mine, both, 0.0).astype(BF)
            scores = lax.dot_general(one, key[:, span], (((1,), (1,)), ((), ())), preferred_element_type=F32)
            scores = 50.0 * jnp.tanh(scores * (1.0 / math.sqrt(HEAD_DIM)) * (1.0 / 50.0))
            expo = jnp.where(allowed, jnp.exp(scores), 0.0)
            weights = (expo / jnp.sum(expo, axis=-1, keepdims=True)).astype(BF)
            parts.append(jnp.dot(weights, value[:, span], preferred_element_type=F32))
        context[:, span] = jnp.where(lane >= HEAD_DIM, parts[1], parts[0]).astype(BF)
    copies[many].wait()
    merged = jnp.dot(context[...], merge[...], preferred_element_type=F32)
    out_ref[...] = (own_ref[...].astype(F32) + merged).astype(BF)


def attended(first, far, near, own, qkv_weight, merge_weight):
    block, width = own.shape
    keys = far.shape[0] + near.shape[0] + block
    padded = -(-keys // 128) * 128
    vmem = pl.BlockSpec(memory_space=pltpu.VMEM)
    return pl.pallas_call(
        attention_kernel,
        in_specs=[pl.BlockSpec(memory_space=pltpu.SMEM)] + [vmem] * 3 + [pl.BlockSpec(memory_space=pl.ANY)] * 2,
        out_specs=vmem,
        out_shape=jax.ShapeDtypeStruct((block, width), BF),
        scratch_shapes=[
            pltpu.VMEM((keys, width), BF),
            pltpu.VMEM((block, width), BF),
            pltpu.VMEM((padded, width), BF),
            pltpu.VMEM((padded, width), BF),
            pltpu.VMEM((block, width), BF),
            pltpu.VMEM((3 * width // 512, width, 512), BF),
            pltpu.VMEM((width, width), BF),
            pltpu.SemaphoreType.DMA((3 * width // 512 + 1,)),
        ],
        compiler_params=pltpu.CompilerParams(vmem_limit_bytes=24 * 2**20),
        cost_estimate=pl.CostEstimate(
            flops=8 * keys * width * width, bytes_accessed=9 * 2**20, transcendentals=2 * HEADS * block * keys
        ),
        name="qkv",
    )(first, far, near, own, *[pltpu.with_memory_space_constraint(w, pltpu.HBM) for w in (qkv_weight, merge_weight)])


def body(frames, qkv_weight, attn_out_weight, head_weight, back_weight):
    rows = frames.shape[0]
    width = frames.shape[1]
    cols = lax.axis_size(COL)
    block = rows * cols
    far = WIN - block
    head_parts = over_time(head_weight)
    back_parts = over_time(back_weight)

    own = column_rows(frames)
    prev = passed_along(own, BLOCKS, 1)
    prev2 = passed_along(own[block - far :], BLOCKS, 2)
    first = lax.axis_index(BLOCKS).astype(jnp.int32)[None] * block
    hidden = attended(first, prev2, prev, own, qkv_weight, attn_out_weight)
    hidden = own_rows_first(hidden)
    unit = root_norm(hidden.astype(F32)).astype(BF)

    every = gathered(from_own(unit), PLANE)
    sent = label_sums(every, head_parts, back_parts)
    summed = jnp.sum(lax.all_to_all(sent, PLANE, 0, 0).astype(F32), axis=0)
    block_totals = jnp.sum(summed[8 * block : 8 * block + 3, :block], axis=0)
    split = three_rows(block_totals.reshape(cols, rows), 128)
    parts = summed[: 8 * block].astype(BF).reshape(8, cols, rows, 128).transpose(1, 0, 2, 3)
    sent = jnp.concatenate([parts.reshape(cols, 8 * rows, 128), split], axis=1)
    summed = column_sum(sent)
    owned_totals = jnp.sum(summed[8 * rows : 8 * rows + 3, :rows], axis=0)
    back_proj = summed[: 8 * rows].reshape(8, rows, 128).transpose(1, 0, 2).reshape(rows, width)
    back_proj = from_own(back_proj) / owned_totals[:, None]

    center = back_proj - jnp.mean(back_proj, axis=-1, keepdims=True)
    spread = jnp.mean(center * center, axis=-1, keepdims=True)
    conditioned = (hidden[:rows].astype(F32) + center * lax.rsqrt(spread + 1e-05)).astype(BF)
    return (conditioned, jnp.log(owned_totals))


def solution(mesh):
    cube = Mesh(mesh.devices.reshape(2, 2, 4, 4, 4), EVERY)
    return jax.shard_map(
        body,
        mesh=cube,
        in_specs=(P(EVERY, None), P(), P(), P(TIME, PLANE + (COL,)), P(PLANE + (COL,), TIME)),
        out_specs=(P(EVERY, None), P(EVERY)),
        check_vma=False,
    )
```

```python
import math

import jax
import jax.numpy as jnp
from jax import lax
from jax.experimental import pallas as pl
from jax.experimental.pallas import tpu as pltpu
from jax.sharding import Mesh, PartitionSpec as P


HEADS = 16
HEAD_DIM = 64
WIN = 128
BF = jnp.bfloat16
F32 = jnp.float32
TIME = ("zl", "c")
PLANE = ("x", "y")
COL = "zh"
BLOCKS = TIME + PLANE
EVERY = BLOCKS + (COL,)


def passed_along(block, axes, distance):
    devices = range(lax.axis_size(axes))
    route = [(i, i + distance) for i in devices if i + distance in devices]
    return lax.ppermute(block, axes, route)


def swapped(block, axis):
    return lax.ppermute(block, axis, [(0, 1), (1, 0)])


def over_time(block):
    beside = swapped(block, "c")
    across = swapped(block, "zl")
    corner = swapped(across, "c")
    return block, beside, across, corner


def from_own(values):
    quarter = values.shape[1] // 4
    q = [values[:, i * quarter : (i + 1) * quarter] for i in range(4)]
    odd = lax.axis_index("c") == 1
    q = [jnp.where(odd, q[i ^ 1], q[i]) for i in range(4)]
    late = lax.axis_index("zl") == 1
    return jnp.concatenate([jnp.where(late, q[i ^ 2], q[i]) for i in range(4)], axis=1)


def turned(block, distance):
    size = lax.axis_size(COL)
    return lax.ppermute(block, COL, [(i, (i + distance) % size) for i in range(size)])


def column_rows(block):
    after = [block, turned(block, -1), turned(block, -2), turned(block, 1)]
    place = lax.axis_index(COL)
    odd = place % 2 == 1
    after = [jnp.where(odd, after[i - 1], after[i]) for i in range(4)]
    late = place >= 2
    return jnp.concatenate([jnp.where(late, after[i - 2], after[i]) for i in range(4)], axis=0)


def column_sum(blocks):
    total = blocks[0].astype(F32)
    for distance in (2, 1, 3):
        block = turned(blocks[distance], distance)
        total = total + block.astype(F32)
    return total


def three_rows(totals, width):
    high = lax.reduce_precision(totals, 8, 7)
    mid = lax.reduce_precision(totals - high, 8, 7)
    low = totals - high - mid
    split = jnp.stack([high, mid, low], axis=1).astype(BF)
    return jnp.pad(split, ((0, 0), (0, 5), (0, width - totals.shape[1])))


def root_norm(values):
    return values * lax.rsqrt(jnp.mean(values * values, axis=-1, keepdims=True) + 1e-06)


STEPS = 4
PARTS = 4


def label_kernel(seen_ref, unit_ref, h0, h1, h2, h3, b0, b1, b2, b3, out_ref, head, back, total, sums, sems):
    step = pl.program_id(0)
    labels = head.shape[1] // PARTS
    count = out_ref.shape[0]
    block = unit_ref.shape[0] // count
    narrow = back.shape[1] // PARTS
    pieces = ((h0, h1, h2, h3), (b0, b1, b2, b3))

    def copies(kind, part):
        span = slice(part * labels, (part + 1) * labels)
        for q in range(PARTS):
            if kind == 0:
                source = pieces[0][q].at[:, span]
                target = head.at[q * 256 : (q + 1) * 256, span]
            else:
                source = pieces[1][q].at[span, :]
                target = back.at[span, q * narrow : (q + 1) * narrow]
            yield pltpu.make_async_copy(source, target, sems.at[kind, part, q])

    @pl.when(step == 0)
    def _():
        for part in range(PARTS):
            for kind in range(2):
                for copy in copies(kind, part):
                    copy.start()

    def arrive(kind, part):
        @pl.when(step == 0)
        def _():
            for copy in copies(kind, part):
                copy.wait()

    def logits(part):
        arrive(0, part)
        span = slice(part * labels, (part + 1) * labels)
        return jnp.dot(unit_ref[...], head[:, span], preferred_element_type=F32)

    ahead = logits(0)
    lanes = None
    for part in range(PARTS):
        now = ahead
        if part + 1 < PARTS:
            ahead = logits(part + 1)
        arrive(1, part)
        probs = jnp.exp(30.0 * jnp.tanh(now * (1.0 / 30.0))).astype(BF)
        wide = probs.astype(F32)
        for k in range(labels // 128):
            column = wide[:, k * 128 : (k + 1) * 128]
            lanes = column if lanes is None else lanes + column
        span = slice(part * labels, (part + 1) * labels)
        value = jnp.dot(probs, back[span, :], preferred_element_type=F32)
        if part == 0:
            total[...] = value
        else:
            total[...] += value
    sums[0 : count * block, :] = lanes
    sums[count * block :, :] = jnp.zeros((sums.shape[0] - count * block, 128), F32)
    row = lax.broadcasted_iota(jnp.int32, (8, 128), 0)
    for s in range(count):
        for j in range(total.shape[1] // 128):
            tile = total[s * block : (s + 1) * block, j * 128 : (j + 1) * 128]
            out_ref[s, j * block : (j + 1) * block, :] = tile.astype(BF)
        flat = jnp.sum(sums[s * block : s * block + 128, :].T, axis=0, keepdims=True)
        high = flat.astype(BF).astype(F32)
        mid = (flat - high).astype(BF).astype(F32)
        low = flat - high - mid
        split = jnp.where(row == 0, high, jnp.where(row == 1, mid, jnp.where(row == 2, low, 0.0)))
        out_ref[s, 8 * block :, :] = split.astype(BF)


def in_hbm(block):
    return pltpu.with_memory_space_constraint(block, pltpu.HBM)


def label_sums(seen, unit, head_parts, back_parts):
    frames, width = unit.shape
    labels = head_parts[0].shape[1]
    slots = 16
    block = frames // slots
    count = slots // STEPS
    rows = 8 * block + 8
    return pl.pallas_call(
        label_kernel,
        grid=(STEPS,),
        in_specs=[pl.BlockSpec(memory_space=pltpu.SMEM), pl.BlockSpec((count * block, width), lambda i: (i, 0))]
        + [pl.BlockSpec(memory_space=pl.ANY)] * 8,
        out_specs=pl.BlockSpec((count, rows, 128), lambda i: (i, 0, 0)),
        out_shape=jax.ShapeDtypeStruct((slots, rows, 128), BF),
        scratch_shapes=[
            pltpu.VMEM((width, labels), BF),
            pltpu.VMEM((labels, width), BF),
            pltpu.VMEM((count * block, width), F32),
            pltpu.VMEM((count * block + 32, 128), F32),
            pltpu.SemaphoreType.DMA((2, PARTS, 4)),
        ],
        compiler_params=pltpu.CompilerParams(vmem_limit_bytes=20 * 2**20),
        cost_estimate=pl.CostEstimate(
            flops=4 * frames * width * labels, bytes_accessed=16 * 2**20, transcendentals=2 * frames * labels
        ),
    )(seen, unit, in_hbm(head_parts[0]), *head_parts[1:], in_hbm(back_parts[0]), *back_parts[1:])


def attention_kernel(place_ref, far_ref, near_ref, own_ref, qkv_ref, merge_ref, out_ref, mine_ref, normed, query, key, value,
                     context, weight, merge, hidden, unit, moved, sems):
    block, width = own_ref.shape
    wide = weight.shape[2]
    many = weight.shape[0]
    copies = [
        pltpu.make_async_copy(qkv_ref.at[:, i * wide : (i + 1) * wide], weight.at[i], sems.at[i])
        for i in range(many)
    ] + [pltpu.make_async_copy(merge_ref, merge, sems.at[many])]
    for copy in copies:
        copy.start()
    past = far_ref.shape[0] + near_ref.shape[0]
    keys = past + block
    row = 0
    for ref in (far_ref, near_ref, own_ref):
        normed[row : row + ref.shape[0], :] = root_norm(ref[...].astype(F32)).astype(BF)
        row += ref.shape[0]
    for i in range(many):
        copies[i].wait()
        part, start = divmod(i * wide, width)
        ref = (query, key, value)[part]
        span = slice(start, start + wide)
        lowest = past if part == 0 else 0
        product = jnp.dot(normed[lowest:keys, :], weight[i], preferred_element_type=F32)
        ref[0 : keys - lowest, span] = product.astype(BF)
        if part:
            ref[keys:, span] = jnp.zeros((ref.shape[0] - keys, wide), BF)
    padded = key.shape[0]
    r = lax.broadcasted_iota(jnp.int32, (block, padded), 0)
    j = lax.broadcasted_iota(jnp.int32, (block, padded), 1)
    allowed = (j <= r + past) & (j > r + past - WIN) & (j < keys) & (place_ref[0] - past + j >= 0)
    lane = lax.broadcasted_iota(jnp.int32, (block, 128), 1)
    for pair in range(width // 128):
        span = slice(pair * 128, (pair + 1) * 128)
        both = query[:, span].astype(F32)
        parts = []
        for side in range(2):
            mine = (lane >= HEAD_DIM) == (side == 1)
            one = jnp.where(mine, both, 0.0).astype(BF)
            scores = lax.dot_general(one, key[:, span], (((1,), (1,)), ((), ())), preferred_element_type=F32)
            scores = 50.0 * jnp.tanh(scores * (1.0 / math.sqrt(HEAD_DIM)) * (1.0 / 50.0))
            expo = jnp.where(allowed, jnp.exp(scores), 0.0)
            weights = (expo / jnp.sum(expo, axis=-1, keepdims=True)).astype(BF)
            parts.append(jnp.dot(weights, value[:, span], preferred_element_type=F32))
        context[:, span] = jnp.where(lane >= HEAD_DIM, parts[1], parts[0]).astype(BF)
    copies[many].wait()
    merged = jnp.dot(context[...], merge[...], preferred_element_type=F32)
    hidden[...] = (own_ref[...].astype(F32) + merged).astype(BF).astype(F32)
    unit[...] = root_norm(hidden[...]).astype(BF).astype(F32)
    rows = mine_ref.shape[0]
    mine_ref[...] = hidden[pl.ds(pl.multiple_of(place_ref[1] * rows, 8), rows), :].astype(BF)
    quarter = width // 4
    for k in range(4):
        row = pl.multiple_of(lax.rem(place_ref[1] + k, 4) * rows, 8)
        for q in range(4):
            column = pl.multiple_of(lax.bitwise_xor(place_ref[2], q) * quarter, quarter)
            piece = unit[pl.ds(row, rows), pl.ds(column, quarter)]
            moved[k * rows : (k + 1) * rows, q * quarter : (q + 1) * quarter] = piece
    spread = moved[...].astype(BF)
    for s in range(out_ref.shape[0]):
        out_ref[s] = spread


def attended(place, far, near, own, qkv_weight, merge_weight, copies):
    block, width = own.shape
    keys = far.shape[0] + near.shape[0] + block
    padded = -(-keys // 128) * 128
    vmem = pl.BlockSpec(memory_space=pltpu.VMEM)
    return pl.pallas_call(
        attention_kernel,
        in_specs=[pl.BlockSpec(memory_space=pltpu.SMEM)] + [vmem] * 3 + [pl.BlockSpec(memory_space=pl.ANY)] * 2,
        out_specs=[vmem, vmem],
        out_shape=[
            jax.ShapeDtypeStruct((copies, block, width), BF),
            jax.ShapeDtypeStruct((block // 4, width), BF),
        ],
        scratch_shapes=[
            pltpu.VMEM((keys, width), BF),
            pltpu.VMEM((block, width), BF),
            pltpu.VMEM((padded, width), BF),
            pltpu.VMEM((padded, width), BF),
            pltpu.VMEM((block, width), BF),
            pltpu.VMEM((3 * width // 512, width, 512), BF),
            pltpu.VMEM((width, width), BF),
            pltpu.VMEM((block, width), F32),
            pltpu.VMEM((block, width), F32),
            pltpu.VMEM((block, width), F32),
            pltpu.SemaphoreType.DMA((3 * width // 512 + 1,)),
        ],
        compiler_params=pltpu.CompilerParams(vmem_limit_bytes=24 * 2**20),
        cost_estimate=pl.CostEstimate(
            flops=8 * keys * width * width, bytes_accessed=9 * 2**20, transcendentals=2 * HEADS * block * keys
        ),
        name="qkv",
    )(place, far, near, own, *[pltpu.with_memory_space_constraint(w, pltpu.HBM) for w in (qkv_weight, merge_weight)])


def body(frames, qkv_weight, attn_out_weight, head_weight, back_weight):
    rows = frames.shape[0]
    width = frames.shape[1]
    cols = lax.axis_size(COL)
    block = rows * cols
    far = WIN - block
    head_parts = over_time(head_weight)
    back_parts = over_time(back_weight)

    own = column_rows(frames)
    prev = passed_along(own, BLOCKS, 1)
    prev2 = passed_along(own[block - far :], BLOCKS, 2)
    place = jnp.stack([lax.axis_index(BLOCKS) * block, lax.axis_index(COL), lax.axis_index(TIME)])
    copies, hidden = attended(
        place.astype(jnp.int32), prev2, prev, own, qkv_weight, attn_out_weight, lax.axis_size(PLANE)
    )
    every = lax.all_to_all(copies, PLANE, 0, 0).reshape(-1, width)
    seen = jnp.max(every[:8, :128].astype(F32), keepdims=True)
    sent = label_sums(seen, every, head_parts, back_parts)
    summed = jnp.sum(lax.all_to_all(sent, PLANE, 0, 0).astype(F32), axis=0)
    block_totals = jnp.sum(summed[8 * block : 8 * block + 3, :block], axis=0)
    split = three_rows(block_totals.reshape(cols, rows), 128)
    parts = summed[: 8 * block].astype(BF).reshape(8, cols, rows, 128).transpose(1, 0, 2, 3)
    sent = jnp.concatenate([parts.reshape(cols, 8 * rows, 128), split], axis=1)
    summed = column_sum(sent)
    owned_totals = jnp.sum(summed[8 * rows : 8 * rows + 3, :rows], axis=0)
    back_proj = summed[: 8 * rows].reshape(8, rows, 128).transpose(1, 0, 2).reshape(rows, width)
    back_proj = from_own(back_proj) / owned_totals[:, None]

    center = back_proj - jnp.mean(back_proj, axis=-1, keepdims=True)
    spread = jnp.mean(center * center, axis=-1, keepdims=True)
    conditioned = (hidden.astype(F32) + center * lax.rsqrt(spread + 1e-05)).astype(BF)
    return (conditioned, jnp.log(owned_totals))


def solution(mesh):
    cube = Mesh(mesh.devices.reshape(2, 2, 4, 4, 4), EVERY)
    return jax.shard_map(
        body,
        mesh=cube,
        in_specs=(P(EVERY, None), P(), P(), P(TIME, PLANE + (COL,)), P(PLANE + (COL,), TIME)),
        out_specs=(P(EVERY, None), P(EVERY)),
        check_vma=False,
    )
```

```python
import math

import jax
import jax.numpy as jnp
from jax import lax
from jax.experimental import pallas as pl
from jax.experimental.pallas import tpu as pltpu
from jax.sharding import Mesh, PartitionSpec as P


HEADS = 16
HEAD_DIM = 64
WIN = 128
BF = jnp.bfloat16
F32 = jnp.float32
TIME = ("zl", "c")
PLANE = ("x", "y")
COL = "zh"
BLOCKS = TIME + PLANE
EVERY = BLOCKS + (COL,)


def gathered(block, axes):
    size = lax.axis_size(axes)
    copies = lax.optimization_barrier(jnp.broadcast_to(block[None], (size,) + block.shape))
    parts = lax.all_to_all(copies, axes, 0, 0)
    return parts.reshape((size * block.shape[0],) + block.shape[1:])


def passed_along(block, axes, distance):
    devices = range(lax.axis_size(axes))
    route = [(i, i + distance) for i in devices if i + distance in devices]
    return lax.ppermute(block, axes, route)


def swapped(block, axis):
    return lax.ppermute(block, axis, [(0, 1), (1, 0)])


def over_time(block):
    beside = swapped(block, "c")
    across = swapped(block, "zl")
    corner = swapped(across, "c")
    return block, beside, across, corner


def from_own(values):
    quarter = values.shape[1] // 4
    q = [values[:, i * quarter : (i + 1) * quarter] for i in range(4)]
    odd = lax.axis_index("c") == 1
    q = [jnp.where(odd, q[i ^ 1], q[i]) for i in range(4)]
    late = lax.axis_index("zl") == 1
    return jnp.concatenate([jnp.where(late, q[i ^ 2], q[i]) for i in range(4)], axis=1)


def turned(block, distance):
    size = lax.axis_size(COL)
    return lax.ppermute(block, COL, [(i, (i + distance) % size) for i in range(size)])


def column_rows(block):
    after = [block, turned(block, -1), turned(block, -2), turned(block, 1)]
    place = lax.axis_index(COL)
    odd = place % 2 == 1
    after = [jnp.where(odd, after[i - 1], after[i]) for i in range(4)]
    late = place >= 2
    return jnp.concatenate([jnp.where(late, after[i - 2], after[i]) for i in range(4)], axis=0)


def own_rows_first(block):
    count = block.shape[0] // 4
    q = [block[i * count : (i + 1) * count] for i in range(4)]
    place = lax.axis_index(COL)
    odd = place % 2 == 1
    q = [jnp.where(odd, q[(i + 1) % 4], q[i]) for i in range(4)]
    late = place >= 2
    return jnp.concatenate([jnp.where(late, q[i - 2], q[i]) for i in range(4)], axis=0)


def column_parts(blocks):
    return [blocks[0]] + [turned(blocks[distance], distance) for distance in (2, 1, 3)]


def finish_kernel(place_ref, p0, p1, p2, p3, hidden_ref, out_ref, log_ref, summed):
    rows, width = hidden_ref.shape
    summed[...] = p0[...].astype(F32) + p1[...].astype(F32) + p2[...].astype(F32) + p3[...].astype(F32)
    groups = width // 128
    last = groups * rows
    total = jnp.sum(summed[last : last + 3, :], axis=0, keepdims=True)
    log_ref[...] = jnp.broadcast_to(jnp.log(total), log_ref.shape)
    column = jnp.broadcast_to(total, (128, 128)).T[:rows, :]
    pieces = []
    for j in range(groups):
        group = lax.bitwise_xor(place_ref[0], j // 2) * 2 + j % 2
        piece = summed[pl.ds(pl.multiple_of(group * rows, 8), rows), :]
        pieces.append(piece / column)
    mean = jnp.sum(sum(pieces), axis=-1, keepdims=True) * (1.0 / width)
    pieces = [piece - mean for piece in pieces]
    spread = jnp.sum(sum(piece * piece for piece in pieces), axis=-1, keepdims=True) * (1.0 / width)
    scale = lax.rsqrt(spread + 1e-05)
    for j in range(groups):
        span = slice(j * 128, (j + 1) * 128)
        out_ref[:, span] = (hidden_ref[:, span].astype(F32) + pieces[j] * scale).astype(BF)


def finished(place, parts, hidden):
    vmem = pl.BlockSpec(memory_space=pltpu.VMEM)
    return pl.pallas_call(
        finish_kernel,
        in_specs=[pl.BlockSpec(memory_space=pltpu.SMEM)] + [vmem] * 5,
        out_specs=[vmem, vmem],
        out_shape=[
            jax.ShapeDtypeStruct(hidden.shape, BF),
            jax.ShapeDtypeStruct((8, 128), F32),
        ],
        scratch_shapes=[pltpu.VMEM(parts[0].shape, F32)],
        compiler_params=pltpu.CompilerParams(vmem_limit_bytes=4 * 2**20),
    )(place, *parts, hidden)


def three_rows(totals, width):
    high = lax.reduce_precision(totals, 8, 7)
    mid = lax.reduce_precision(totals - high, 8, 7)
    low = totals - high - mid
    split = jnp.stack([high, mid, low], axis=1).astype(BF)
    return jnp.pad(split, ((0, 0), (0, 5), (0, width - totals.shape[1])))


def root_norm(values):
    return values * lax.rsqrt(jnp.mean(values * values, axis=-1, keepdims=True) + 1e-06)


STEPS = 4
PARTS = 4


def label_kernel(unit_ref, h0, h1, h2, h3, b0, b1, b2, b3, out_ref, head, back, total, sums, sems):
    step = pl.program_id(0)
    labels = head.shape[1] // PARTS
    count = out_ref.shape[0]
    block = unit_ref.shape[0] // count
    narrow = back.shape[1] // PARTS
    pieces = ((h0, h1, h2, h3), (b0, b1, b2, b3))

    def copies(kind, part):
        span = slice(part * labels, (part + 1) * labels)
        for q in range(PARTS):
            if kind == 0:
                source = pieces[0][q].at[:, span]
                target = head.at[q * 256 : (q + 1) * 256, span]
            else:
                source = pieces[1][q].at[span, :]
                target = back.at[span, q * narrow : (q + 1) * narrow]
            yield pltpu.make_async_copy(source, target, sems.at[kind, part, q])

    @pl.when(step == 0)
    def _():
        for part in range(PARTS):
            for kind in range(2):
                for copy in copies(kind, part):
                    copy.start()

    def arrive(kind, part):
        @pl.when(step == 0)
        def _():
            for copy in copies(kind, part):
                copy.wait()

    def logits(part):
        arrive(0, part)
        span = slice(part * labels, (part + 1) * labels)
        return jnp.dot(unit_ref[...], head[:, span], preferred_element_type=F32)

    ahead = logits(0)
    lanes = None
    for part in range(PARTS):
        now = ahead
        if part + 1 < PARTS:
            ahead = logits(part + 1)
        arrive(1, part)
        probs = jnp.exp(30.0 * jnp.tanh(now * (1.0 / 30.0))).astype(BF)
        wide = probs.astype(F32)
        for k in range(labels // 128):
            column = wide[:, k * 128 : (k + 1) * 128]
            lanes = column if lanes is None else lanes + column
        span = slice(part * labels, (part + 1) * labels)
        value = jnp.dot(probs, back[span, :], preferred_element_type=F32)
        if part == 0:
            total[...] = value
        else:
            total[...] += value
    sums[0 : count * block, :] = lanes
    sums[count * block :, :] = jnp.zeros((sums.shape[0] - count * block, 128), F32)
    row = lax.broadcasted_iota(jnp.int32, (8, 128), 0)
    for s in range(count):
        for j in range(total.shape[1] // 128):
            tile = total[s * block : (s + 1) * block, j * 128 : (j + 1) * 128]
            out_ref[s, j * block : (j + 1) * block, :] = tile.astype(BF)
        flat = jnp.sum(sums[s * block : s * block + 128, :].T, axis=0, keepdims=True)
        high = flat.astype(BF).astype(F32)
        mid = (flat - high).astype(BF).astype(F32)
        low = flat - high - mid
        split = jnp.where(row == 0, high, jnp.where(row == 1, mid, jnp.where(row == 2, low, 0.0)))
        out_ref[s, 8 * block :, :] = split.astype(BF)


def label_sums(unit, head_parts, back_parts):
    frames, width = unit.shape
    labels = head_parts[0].shape[1]
    slots = 16
    block = frames // slots
    count = slots // STEPS
    rows = 8 * block + 8
    return pl.pallas_call(
        label_kernel,
        grid=(STEPS,),
        in_specs=[pl.BlockSpec((count * block, width), lambda i: (i, 0))]
        + [pl.BlockSpec(memory_space=pltpu.HBM)] * 8,
        out_specs=pl.BlockSpec((count, rows, 128), lambda i: (i, 0, 0)),
        out_shape=jax.ShapeDtypeStruct((slots, rows, 128), BF),
        scratch_shapes=[
            pltpu.VMEM((width, labels), BF),
            pltpu.VMEM((labels, width), BF),
            pltpu.VMEM((count * block, width), F32),
            pltpu.VMEM((count * block + 32, 128), F32),
            pltpu.SemaphoreType.DMA((2, PARTS, 4)),
        ],
        compiler_params=pltpu.CompilerParams(vmem_limit_bytes=20 * 2**20),
        cost_estimate=pl.CostEstimate(
            flops=4 * frames * width * labels, bytes_accessed=16 * 2**20, transcendentals=2 * frames * labels
        ),
    )(unit, *[pltpu.with_memory_space_constraint(p, pltpu.HBM) for p in (*head_parts, *back_parts)])


def attention_kernel(first_ref, far_ref, near_ref, own_ref, qkv_ref, merge_ref, out_ref, normed, query, key, value, context,
                     weight, merge, sems):
    block, width = own_ref.shape
    wide = weight.shape[2]
    many = weight.shape[0]
    copies = [
        pltpu.make_async_copy(qkv_ref.at[:, i * wide : (i + 1) * wide], weight.at[i], sems.at[i])
        for i in range(many)
    ] + [pltpu.make_async_copy(merge_ref, merge, sems.at[many])]
    for copy in copies:
        copy.start()
    past = far_ref.shape[0] + near_ref.shape[0]
    keys = past + block
    row = 0
    for ref in (far_ref, near_ref, own_ref):
        normed[row : row + ref.shape[0], :] = root_norm(ref[...].astype(F32)).astype(BF)
        row += ref.shape[0]
    for i in range(many):
        copies[i].wait()
        part, start = divmod(i * wide, width)
        ref = (query, key, value)[part]
        span = slice(start, start + wide)
        lowest = past if part == 0 else 0
        product = jnp.dot(normed[lowest:keys, :], weight[i], preferred_element_type=F32)
        ref[0 : keys - lowest, span] = product.astype(BF)
        if part:
            ref[keys:, span] = jnp.zeros((ref.shape[0] - keys, wide), BF)
    padded = key.shape[0]
    r = lax.broadcasted_iota(jnp.int32, (block, padded), 0)
    j = lax.broadcasted_iota(jnp.int32, (block, padded), 1)
    allowed = (j <= r + past) & (j > r + past - WIN) & (j < keys) & (first_ref[0] - past + j >= 0)
    lane = lax.broadcasted_iota(jnp.int32, (block, 128), 1)
    for pair in range(width // 128):
        span = slice(pair * 128, (pair + 1) * 128)
        both = query[:, span].astype(F32)
        parts = []
        for side in range(2):
            mine = (lane >= HEAD_DIM) == (side == 1)
            one = jnp.where(mine, both, 0.0).astype(BF)
            scores = lax.dot_general(one, key[:, span], (((1,), (1,)), ((), ())), preferred_element_type=F32)
            scores = 50.0 * jnp.tanh(scores * (1.0 / math.sqrt(HEAD_DIM)) * (1.0 / 50.0))
            expo = jnp.where(allowed, jnp.exp(scores), 0.0)
            weights = (expo / jnp.sum(expo, axis=-1, keepdims=True)).astype(BF)
            parts.append(jnp.dot(weights, value[:, span], preferred_element_type=F32))
        context[:, span] = jnp.where(lane >= HEAD_DIM, parts[1], parts[0]).astype(BF)
    copies[many].wait()
    merged = jnp.dot(context[...], merge[...], preferred_element_type=F32)
    out_ref[...] = (own_ref[...].astype(F32) + merged).astype(BF)


def attended(first, far, near, own, qkv_weight, merge_weight):
    block, width = own.shape
    keys = far.shape[0] + near.shape[0] + block
    padded = -(-keys // 128) * 128
    vmem = pl.BlockSpec(memory_space=pltpu.VMEM)
    return pl.pallas_call(
        attention_kernel,
        in_specs=[pl.BlockSpec(memory_space=pltpu.SMEM)] + [vmem] * 3 + [pl.BlockSpec(memory_space=pl.ANY)] * 2,
        out_specs=vmem,
        out_shape=jax.ShapeDtypeStruct((block, width), BF),
        scratch_shapes=[
            pltpu.VMEM((keys, width), BF),
            pltpu.VMEM((block, width), BF),
            pltpu.VMEM((padded, width), BF),
            pltpu.VMEM((padded, width), BF),
            pltpu.VMEM((block, width), BF),
            pltpu.VMEM((3 * width // 512, width, 512), BF),
            pltpu.VMEM((width, width), BF),
            pltpu.SemaphoreType.DMA((3 * width // 512 + 1,)),
        ],
        compiler_params=pltpu.CompilerParams(vmem_limit_bytes=24 * 2**20),
        cost_estimate=pl.CostEstimate(
            flops=8 * keys * width * width, bytes_accessed=9 * 2**20, transcendentals=2 * HEADS * block * keys
        ),
        name="qkv",
    )(first, far, near, own, *[pltpu.with_memory_space_constraint(w, pltpu.HBM) for w in (qkv_weight, merge_weight)])


def body(frames, qkv_weight, attn_out_weight, head_weight, back_weight):
    rows = frames.shape[0]
    cols = lax.axis_size(COL)
    block = rows * cols
    far = WIN - block
    head_parts = over_time(head_weight)
    back_parts = over_time(back_weight)

    own = column_rows(frames)
    prev = passed_along(own, BLOCKS, 1)
    prev2 = passed_along(own[block - far :], BLOCKS, 2)
    first = lax.axis_index(BLOCKS).astype(jnp.int32)[None] * block
    hidden = attended(first, prev2, prev, own, qkv_weight, attn_out_weight)
    hidden = own_rows_first(hidden)
    unit = root_norm(hidden.astype(F32)).astype(BF)

    every = gathered(from_own(unit), PLANE)
    sent = label_sums(every, head_parts, back_parts)
    summed = jnp.sum(lax.all_to_all(sent, PLANE, 0, 0).astype(F32), axis=0)
    block_totals = jnp.sum(summed[8 * block : 8 * block + 3, :block], axis=0)
    split = three_rows(block_totals.reshape(cols, rows), 128)
    parts = summed[: 8 * block].astype(BF).reshape(8, cols, rows, 128).transpose(1, 0, 2, 3)
    sent = jnp.concatenate([parts.reshape(cols, 8 * rows, 128), split], axis=1)
    place = lax.axis_index(TIME).astype(jnp.int32)[None]
    conditioned, logs = finished(place, column_parts(sent), hidden[:rows])
    return (conditioned, logs[0, :rows])


def solution(mesh):
    cube = Mesh(mesh.devices.reshape(2, 2, 4, 4, 4), EVERY)
    return jax.shard_map(
        body,
        mesh=cube,
        in_specs=(P(EVERY, None), P(), P(), P(TIME, PLANE + (COL,)), P(PLANE + (COL,), TIME)),
        out_specs=(P(EVERY, None), P(EVERY)),
        check_vma=False,
    )
```

```python
import math

import jax
import jax.numpy as jnp
from jax import lax
from jax.experimental import pallas as pl
from jax.experimental.pallas import tpu as pltpu
from jax.sharding import Mesh, PartitionSpec as P


HEADS = 16
HEAD_DIM = 64
WIN = 128
BF = jnp.bfloat16
F32 = jnp.float32
TIME = ("zl", "c")
PLANE = ("x", "y")
COL = "zh"
BLOCKS = TIME + PLANE
EVERY = BLOCKS + (COL,)


def gathered(block, axes):
    size = lax.axis_size(axes)
    copies = lax.optimization_barrier(jnp.broadcast_to(block[None], (size,) + block.shape))
    parts = lax.all_to_all(copies, axes, 0, 0)
    return parts.reshape((size * block.shape[0],) + block.shape[1:])


def passed_along(block, axes, distance):
    devices = range(lax.axis_size(axes))
    route = [(i, i + distance) for i in devices if i + distance in devices]
    return lax.ppermute(block, axes, route)


def swapped(block, axis):
    return lax.ppermute(block, axis, [(0, 1), (1, 0)])


def over_time(block):
    beside = swapped(block, "c")
    across = swapped(block, "zl")
    corner = swapped(across, "c")
    return block, beside, across, corner


def from_own(values):
    quarter = values.shape[1] // 4
    q = [values[:, i * quarter : (i + 1) * quarter] for i in range(4)]
    odd = lax.axis_index("c") == 1
    q = [jnp.where(odd, q[i ^ 1], q[i]) for i in range(4)]
    late = lax.axis_index("zl") == 1
    return jnp.concatenate([jnp.where(late, q[i ^ 2], q[i]) for i in range(4)], axis=1)


def turned(block, distance):
    size = lax.axis_size(COL)
    return lax.ppermute(block, COL, [(i, (i + distance) % size) for i in range(size)])


def column_rows(block):
    after = [block, turned(block, -1), turned(block, -2), turned(block, 1)]
    place = lax.axis_index(COL)
    odd = place % 2 == 1
    after = [jnp.where(odd, after[i - 1], after[i]) for i in range(4)]
    late = place >= 2
    return jnp.concatenate([jnp.where(late, after[i - 2], after[i]) for i in range(4)], axis=0)


def own_rows_first(block):
    count = block.shape[0] // 4
    q = [block[i * count : (i + 1) * count] for i in range(4)]
    place = lax.axis_index(COL)
    odd = place % 2 == 1
    q = [jnp.where(odd, q[(i + 1) % 4], q[i]) for i in range(4)]
    late = place >= 2
    return jnp.concatenate([jnp.where(late, q[i - 2], q[i]) for i in range(4)], axis=0)


def column_parts(blocks):
    return [blocks[0]] + [turned(blocks[distance], distance) for distance in (2, 1, 3)]


def finish_kernel(place_ref, p0, p1, p2, p3, hidden_ref, out_ref, log_ref, summed):
    rows, width = hidden_ref.shape
    summed[...] = p0[...].astype(F32) + p1[...].astype(F32) + p2[...].astype(F32) + p3[...].astype(F32)
    groups = width // 128
    last = groups * rows
    total = jnp.sum(summed[last : last + 3, :], axis=0, keepdims=True)
    log_ref[...] = jnp.broadcast_to(jnp.log(total), log_ref.shape)
    column = jnp.broadcast_to(total, (128, 128)).T[:rows, :]
    pieces = []
    for j in range(groups):
        group = lax.bitwise_xor(place_ref[0], j // 2) * 2 + j % 2
        piece = summed[pl.ds(pl.multiple_of(group * rows, 8), rows), :]
        pieces.append(piece / column)
    mean = jnp.sum(sum(pieces), axis=-1, keepdims=True) * (1.0 / width)
    pieces = [piece - mean for piece in pieces]
    spread = jnp.sum(sum(piece * piece for piece in pieces), axis=-1, keepdims=True) * (1.0 / width)
    scale = lax.rsqrt(spread + 1e-05)
    for j in range(groups):
        span = slice(j * 128, (j + 1) * 128)
        out_ref[:, span] = (hidden_ref[:, span].astype(F32) + pieces[j] * scale).astype(BF)


def finished(place, parts, hidden):
    vmem = pl.BlockSpec(memory_space=pltpu.VMEM)
    return pl.pallas_call(
        finish_kernel,
        in_specs=[pl.BlockSpec(memory_space=pltpu.SMEM)] + [vmem] * 5,
        out_specs=[vmem, vmem],
        out_shape=[
            jax.ShapeDtypeStruct(hidden.shape, BF),
            jax.ShapeDtypeStruct((8, 128), F32),
        ],
        scratch_shapes=[pltpu.VMEM(parts[0].shape, F32)],
        compiler_params=pltpu.CompilerParams(vmem_limit_bytes=4 * 2**20),
    )(place, *parts, hidden)


def three_rows(totals, width):
    high = lax.reduce_precision(totals, 8, 7)
    mid = lax.reduce_precision(totals - high, 8, 7)
    low = totals - high - mid
    split = jnp.stack([high, mid, low], axis=1).astype(BF)
    return jnp.pad(split, ((0, 0), (0, 5), (0, width - totals.shape[1])))


def root_norm(values):
    return values * lax.rsqrt(jnp.mean(values * values, axis=-1, keepdims=True) + 1e-06)


STEPS = 4
PARTS = 4


def label_kernel(unit_ref, h0, h1, h2, h3, b0, b1, b2, b3, out_ref, head, back, total, sums, sems):
    labels = head.shape[1] // PARTS
    count = out_ref.shape[0] // STEPS
    block = unit_ref.shape[0] // out_ref.shape[0]
    narrow = back.shape[1] // PARTS
    pieces = ((h0, h1, h2, h3), (b0, b1, b2, b3))

    def copies(kind, part):
        span = slice(part * labels, (part + 1) * labels)
        for q in range(PARTS):
            if kind == 0:
                source = pieces[0][q].at[:, span]
                target = head.at[q * 256 : (q + 1) * 256, span]
            else:
                source = pieces[1][q].at[span, :]
                target = back.at[span, q * narrow : (q + 1) * narrow]
            yield pltpu.make_async_copy(source, target, sems.at[kind, part, q])

    for part in range(PARTS):
        for kind in range(2):
            for copy in copies(kind, part):
                copy.start()

    @pl.loop(0, STEPS)
    def _(step):
        label_step(step, count, block, labels, copies, unit_ref, out_ref, head, back, total, sums)


def label_step(step, count, block, labels, copies, unit_ref, out_ref, head, back, total, sums):
    frames = pl.ds(pl.multiple_of(step * (count * block), 128), count * block)

    def arrive(kind, part):
        @pl.when(step == 0)
        def _():
            for copy in copies(kind, part):
                copy.wait()

    def logits(part):
        arrive(0, part)
        span = slice(part * labels, (part + 1) * labels)
        return jnp.dot(unit_ref[frames, :], head[:, span], preferred_element_type=F32)

    ahead = logits(0)
    lanes = None
    for part in range(PARTS):
        now = ahead
        if part + 1 < PARTS:
            ahead = logits(part + 1)
        arrive(1, part)
        probs = jnp.exp(30.0 * jnp.tanh(now * (1.0 / 30.0))).astype(BF)
        wide = probs.astype(F32)
        for k in range(labels // 128):
            column = wide[:, k * 128 : (k + 1) * 128]
            lanes = column if lanes is None else lanes + column
        span = slice(part * labels, (part + 1) * labels)
        value = jnp.dot(probs, back[span, :], preferred_element_type=F32)
        if part == 0:
            total[...] = value
        else:
            total[...] += value
    sums[0 : count * block, :] = lanes
    sums[count * block :, :] = jnp.zeros((sums.shape[0] - count * block, 128), F32)
    row = lax.broadcasted_iota(jnp.int32, (8, 128), 0)
    for s in range(count):
        for j in range(total.shape[1] // 128):
            tile = total[s * block : (s + 1) * block, j * 128 : (j + 1) * 128]
            out_ref[step * count + s, j * block : (j + 1) * block, :] = tile.astype(BF)
        flat = jnp.sum(sums[s * block : s * block + 128, :].T, axis=0, keepdims=True)
        high = flat.astype(BF).astype(F32)
        mid = (flat - high).astype(BF).astype(F32)
        low = flat - high - mid
        split = jnp.where(row == 0, high, jnp.where(row == 1, mid, jnp.where(row == 2, low, 0.0)))
        out_ref[step * count + s, 8 * block :, :] = split.astype(BF)


def label_sums(unit, head_parts, back_parts):
    frames, width = unit.shape
    labels = head_parts[0].shape[1]
    slots = 16
    block = frames // slots
    count = slots // STEPS
    rows = 8 * block + 8
    return pl.pallas_call(
        label_kernel,
        in_specs=[pl.BlockSpec(memory_space=pltpu.VMEM)]
        + [pl.BlockSpec(memory_space=pltpu.HBM)] * 8,
        out_specs=pl.BlockSpec(memory_space=pltpu.VMEM),
        out_shape=jax.ShapeDtypeStruct((slots, rows, 128), BF),
        scratch_shapes=[
            pltpu.VMEM((width, labels), BF),
            pltpu.VMEM((labels, width), BF),
            pltpu.VMEM((count * block, width), F32),
            pltpu.VMEM((count * block + 32, 128), F32),
            pltpu.SemaphoreType.DMA((2, PARTS, 4)),
        ],
        compiler_params=pltpu.CompilerParams(vmem_limit_bytes=20 * 2**20),
        cost_estimate=pl.CostEstimate(
            flops=4 * frames * width * labels, bytes_accessed=16 * 2**20, transcendentals=2 * frames * labels
        ),
    )(unit, *[pltpu.with_memory_space_constraint(p, pltpu.HBM) for p in (*head_parts, *back_parts)])


def attention_kernel(first_ref, far_ref, near_ref, own_ref, qkv_ref, merge_ref, out_ref, normed, query, key, value, context,
                     weight, merge, sems):
    block, width = own_ref.shape
    wide = weight.shape[2]
    many = weight.shape[0]
    copies = [
        pltpu.make_async_copy(qkv_ref.at[:, i * wide : (i + 1) * wide], weight.at[i], sems.at[i])
        for i in range(many)
    ] + [pltpu.make_async_copy(merge_ref, merge, sems.at[many])]
    for copy in copies:
        copy.start()
    past = far_ref.shape[0] + near_ref.shape[0]
    keys = past + block
    row = 0
    for ref in (far_ref, near_ref, own_ref):
        normed[row : row + ref.shape[0], :] = root_norm(ref[...].astype(F32)).astype(BF)
        row += ref.shape[0]
    for i in range(many):
        copies[i].wait()
        part, start = divmod(i * wide, width)
        ref = (query, key, value)[part]
        span = slice(start, start + wide)
        lowest = past if part == 0 else 0
        product = jnp.dot(normed[lowest:keys, :], weight[i], preferred_element_type=F32)
        ref[0 : keys - lowest, span] = product.astype(BF)
        if part:
            ref[keys:, span] = jnp.zeros((ref.shape[0] - keys, wide), BF)
    padded = key.shape[0]
    r = lax.broadcasted_iota(jnp.int32, (block, padded), 0)
    j = lax.broadcasted_iota(jnp.int32, (block, padded), 1)
    allowed = (j <= r + past) & (j > r + past - WIN) & (j < keys) & (first_ref[0] - past + j >= 0)
    lane = lax.broadcasted_iota(jnp.int32, (block, 128), 1)
    for pair in range(width // 128):
        span = slice(pair * 128, (pair + 1) * 128)
        both = query[:, span].astype(F32)
        parts = []
        for side in range(2):
            mine = (lane >= HEAD_DIM) == (side == 1)
            one = jnp.where(mine, both, 0.0).astype(BF)
            scores = lax.dot_general(one, key[:, span], (((1,), (1,)), ((), ())), preferred_element_type=F32)
            scores = 50.0 * jnp.tanh(scores * (1.0 / math.sqrt(HEAD_DIM)) * (1.0 / 50.0))
            expo = jnp.where(allowed, jnp.exp(scores), 0.0)
            weights = (expo / jnp.sum(expo, axis=-1, keepdims=True)).astype(BF)
            parts.append(jnp.dot(weights, value[:, span], preferred_element_type=F32))
        context[:, span] = jnp.where(lane >= HEAD_DIM, parts[1], parts[0]).astype(BF)
    copies[many].wait()
    merged = jnp.dot(context[...], merge[...], preferred_element_type=F32)
    out_ref[...] = (own_ref[...].astype(F32) + merged).astype(BF)


def attended(first, far, near, own, qkv_weight, merge_weight):
    block, width = own.shape
    keys = far.shape[0] + near.shape[0] + block
    padded = -(-keys // 128) * 128
    vmem = pl.BlockSpec(memory_space=pltpu.VMEM)
    return pl.pallas_call(
        attention_kernel,
        in_specs=[pl.BlockSpec(memory_space=pltpu.SMEM)] + [vmem] * 3 + [pl.BlockSpec(memory_space=pl.ANY)] * 2,
        out_specs=vmem,
        out_shape=jax.ShapeDtypeStruct((block, width), BF),
        scratch_shapes=[
            pltpu.VMEM((keys, width), BF),
            pltpu.VMEM((block, width), BF),
            pltpu.VMEM((padded, width), BF),
            pltpu.VMEM((padded, width), BF),
            pltpu.VMEM((block, width), BF),
            pltpu.VMEM((3 * width // 512, width, 512), BF),
            pltpu.VMEM((width, width), BF),
            pltpu.SemaphoreType.DMA((3 * width // 512 + 1,)),
        ],
        compiler_params=pltpu.CompilerParams(vmem_limit_bytes=24 * 2**20),
        cost_estimate=pl.CostEstimate(
            flops=8 * keys * width * width, bytes_accessed=9 * 2**20, transcendentals=2 * HEADS * block * keys
        ),
        name="qkv",
    )(first, far, near, own, *[pltpu.with_memory_space_constraint(w, pltpu.HBM) for w in (qkv_weight, merge_weight)])


def body(frames, qkv_weight, attn_out_weight, head_weight, back_weight):
    rows = frames.shape[0]
    cols = lax.axis_size(COL)
    block = rows * cols
    far = WIN - block
    head_parts = over_time(head_weight)
    back_parts = over_time(back_weight)

    own = column_rows(frames)
    prev = passed_along(own, BLOCKS, 1)
    prev2 = passed_along(own[block - far :], BLOCKS, 2)
    first = lax.axis_index(BLOCKS).astype(jnp.int32)[None] * block
    hidden = attended(first, prev2, prev, own, qkv_weight, attn_out_weight)
    hidden = own_rows_first(hidden)
    unit = root_norm(hidden.astype(F32)).astype(BF)

    every = gathered(from_own(unit), PLANE)
    sent = label_sums(every, head_parts, back_parts)
    summed = jnp.sum(lax.all_to_all(sent, PLANE, 0, 0).astype(F32), axis=0)
    block_totals = jnp.sum(summed[8 * block : 8 * block + 3, :block], axis=0)
    split = three_rows(block_totals.reshape(cols, rows), 128)
    parts = summed[: 8 * block].astype(BF).reshape(8, cols, rows, 128).transpose(1, 0, 2, 3)
    sent = jnp.concatenate([parts.reshape(cols, 8 * rows, 128), split], axis=1)
    place = lax.axis_index(TIME).astype(jnp.int32)[None]
    conditioned, logs = finished(place, column_parts(sent), hidden[:rows])
    return (conditioned, logs[0, :rows])


def solution(mesh):
    cube = Mesh(mesh.devices.reshape(2, 2, 4, 4, 4), EVERY)
    return jax.shard_map(
        body,
        mesh=cube,
        in_specs=(P(EVERY, None), P(), P(), P(TIME, PLANE + (COL,)), P(PLANE + (COL,), TIME)),
        out_specs=(P(EVERY, None), P(EVERY)),
        check_vma=False,
    )
```
